32 devices in a mesh: field: 2 (over y), ccd: 16 (over z, x, core).
Axes of the slice: x: 2, y: 2, z: 4, core: 2. Of those that a mesh axis runs over, the one named last changes fastest.
Arguments:
- exposures: float32 [2, 4096, 1024], P(None, ('field', 'ccd')), parts along dimension 1, may hold values from -100 to 100
- lanczos_shift: int32 [2, 32, 2], P(None, ('field', 'ccd')), parts along dimension 1, may hold values from -2 to 2
- lanczos_frac: float32 [2, 32, 2], P(None, ('field', 'ccd')), parts along dimension 1, may hold values from 0 to 1
- margin_patch: int32 [32, 32, 1], P('field'), parts along dimension 0, may hold values from 0 to 15; in each aligned block of 32 rows (0 to 31, 32 to 63, ..., all dimensions but the last counted through in order) at most 4 rows name the same one
- margin_slot: int32 [32, 32], P('field'), parts along dimension 0, may hold values from 0 to 31
Outputs:
- difference: float32 [4096, 1024], P(('field', 'ccd')), parts along dimension 0
The draws below stay inside these ranges and needn't reach their ends.
There are 2 independent parts, one for each index of `field`. The reference program is written for one: setup_inputs(seed, part) draws one part's arguments, and reference() takes and returns one part's arrays. A program takes and returns all parts, laid end to end along the dimension named above; each array names one. Nothing has to cross between parts.
Inputs may be any that keep to these rules, and one draw needn't show every extreme that they name: `margin_patch`: no CCD has more than 4 of its blocks on one patch, and some CCD has exactly 4 on one patch; every patch is intersected by some block.
All inputs are finite; a program needn't handle non-finite values.
Results may differ from the reference program's by a relative error of at most 0.0003.
Values sent between devices are 32-bit elements; how exact they have to be, the bound alone decides.
No kernel may reach another device: no remote copies, remote signals or barrier semaphores. Data moves between devices by JAX's collectives and lax.ppermute only.
A program may use at most 128 MiB of HBM per device.

```python
import math
import jax
import jax.numpy as jnp
import numpy as np
from jax import lax

TR = 128
TC = 1024
BR = 32
BC = 128
KSIDE = 5
KB = 25
NB = 32
NCCD = 16
CAP = 4


def draw_exposures(key, part):
    key_sky, key_gain, key_noise = jax.random.split(jax.random.fold_in(key, 71), 3)
    sky = jnp.clip(jax.random.normal(key_sky, (NCCD, TR, TC), jnp.float32), -6.0, 6.0)
    sides = jnp.roll(sky, 1, 1) + jnp.roll(sky, -1, 1) + jnp.roll(sky, 1, 2) + jnp.roll(sky, -1, 2)
    corners = jnp.roll(jnp.roll(sky, 1, 1), 1, 2) + jnp.roll(jnp.roll(sky, 1, 1), -1, 2)
    corners = corners + jnp.roll(jnp.roll(sky, -1, 1), 1, 2) + jnp.roll(jnp.roll(sky, -1, 1), -1, 2)
    blurred = 0.25 * sky + 0.125 * sides + 0.0625 * corners
    ramp = 1.0 + 2.0 * jnp.arange(NCCD).astype(jnp.float32) / max(NCCD - 1, 1)
    gains = ramp[:, None, None] * jax.random.uniform(key_gain, (NCCD, 1, 1), jnp.float32, 0.8, 1.2)
    noise = 0.5 * jnp.clip(jax.random.normal(key_noise, (NCCD, TR, TC), jnp.float32), -6.0, 6.0)
    science = gains * blurred + noise
    return jnp.stack([sky, science]).reshape(2, NCCD * TR, TC).astype(jnp.float32)


def place_ends(entries, key, least, largest):
    place = [jax.random.randint(jax.random.fold_in(key, axis), (), 0, length) for axis, length in enumerate(entries.shape)]
    widest = entries.shape.index(max(entries.shape))
    beside = place[:widest] + [(place[widest] + 1) % entries.shape[widest]] + place[widest + 1:]
    return entries.at[tuple(place)].set(least).at[tuple(beside)].set(largest)


def level_of(rng, dims, cuts, low, top_value):
    gain, own = 1.0, jax.random.fold_in(rng, 6)
    for dim, parts in cuts:
        heights = jnp.exp(jax.random.uniform(jax.random.fold_in(own, dim), (parts,), jnp.float32, low / len(cuts), top_value / len(cuts)))
        gain = gain * jnp.repeat(heights, dims[dim] // parts).reshape([-1 if axis == dim else 1 for axis in range(len(dims))])
    return gain


def routed_block(stream_key, own, number, rows, amount, top, most, skew):
    order = jax.random.permutation(stream_key, amount)
    heavy_load, common = portions_of(amount, rows * top, most, skew, True), portions_of(amount, rows * top, most, skew, False)
    places = jnp.arange(amount)

    def named(lengths, turn):
        used = int((lengths > 0).sum())
        fixed = max(1, used // 4)
        passed = fixed + (places - fixed + turn * (used - fixed)) % max(1, amount - fixed)
        return jnp.zeros((amount,), jnp.int32).at[order[jnp.where(places < fixed, places, passed)]].set(jnp.asarray(lengths, jnp.int32))

    lengths = jnp.where(number % 4 == 0, named(heavy_load, number // 4), named(common, number - number // 4 - 1))
    mixed = jax.random.permutation(jax.random.fold_in(own, 3), amount)
    donor, receiver = mixed[0:amount // 2 * 2:2], mixed[1:amount // 2 * 2:2]
    room = jnp.minimum(lengths[donor] - 1, most - lengths[receiver]) // 2
    room = jnp.where((donor == order[0]) | (receiver == order[0]) | (lengths[receiver] == 0), 0, jnp.maximum(room, 0))
    passed = jax.random.randint(jax.random.fold_in(own, 4), (amount // 2,), 0, 1 << 20) % (room + 1)
    lengths = lengths.at[donor].add(-passed).at[receiver].add(passed)
    members = jnp.searchsorted(jnp.cumsum(lengths), jnp.arange(rows * top), side="right").astype(jnp.int32)
    table = members.reshape(top, rows).T
    table = table[jax.random.permutation(jax.random.fold_in(own, 1), rows)]
    turn = jax.random.randint(jax.random.fold_in(own, 2), (rows, 1), 0, top)
    return jnp.take_along_axis(table, (jnp.arange(top)[None, :] + turn) % top, axis=1)


def portions_of(number_of, total, most, lean, full):
    weights = [(1 << 20) // math.isqrt(standing ** lean) + 1 for standing in range(1, number_of + 1)]
    largest = most if full else min(most, max(-(-total // number_of), total * weights[0] // sum(weights)))
    least = 1 if total - largest >= number_of - 1 else 0
    given, spare = [largest] + [least] * (number_of - 1), total - largest - least * (number_of - 1)
    while spare > 0:
        movable = [i for i in range(1, number_of) if given[i] < largest] or [i for i in range(1, number_of) if given[i] < most]
        whole, remaining = sum([weights[i] for i in movable]), spare
        for i in movable:
            extra = min(most - given[i], max(1, remaining * weights[i] // whole), spare)
            given[i] = given[i] + extra
            spare = spare - extra
    return np.array(given)


def setup_inputs(seed: int = 0, part: int = 0) -> dict:
    key_list = jax.random.split(jax.random.key(seed), 6)
    part_keys = jax.random.split(jax.random.fold_in(key_list[5], part), 6)
    exposures = draw_exposures(jax.random.fold_in(jax.random.fold_in(key_list[5], part), 71), part)
    lanczos_shift = place_ends(jax.random.randint(part_keys[1], (2, NCCD, 2), -2, 3), jax.random.fold_in(part_keys[1], 1), -2, 2).astype(jnp.int32)
    lanczos_frac = jnp.clip(1.0 * jax.random.uniform(part_keys[2], (2, NCCD, 2), jnp.float32) ** level_of(part_keys[2], (2, NCCD, 2), ((1, 16),), -0.2, 0.2), 0.0, 1.0)
    margin_patch_keys = jax.random.split(jax.random.fold_in(part_keys[3], 1), NCCD * NB // NB)
    margin_patch_turns = jax.random.permutation(jax.random.fold_in(part_keys[3], 3), NCCD * NB // NB)
    margin_patch = jax.vmap(lambda own, number: routed_block(jax.random.fold_in(part_keys[3], 2), own, number, NB, NCCD, 1, CAP, 2))(margin_patch_keys, margin_patch_turns).reshape((NCCD, NB, 1))
    margin_slot = place_ends(jax.random.randint(part_keys[4], (NCCD, NB), 0, NB), jax.random.fold_in(part_keys[4], 1), 0, NB - 1).astype(jnp.int32)
    return dict(exposures=exposures, lanczos_shift=lanczos_shift, lanczos_frac=lanczos_frac, margin_patch=margin_patch, margin_slot=margin_slot)


def lanczos_matrix(length, shift, frac):
    positions = jnp.arange(length).astype(jnp.float32)
    offset = positions[None, :] - positions[:, None] - shift.astype(jnp.float32) - frac
    taper = jnp.sinc(offset) * jnp.sinc(offset / 3.0)
    return jnp.where(jnp.abs(offset) < 3.0, taper, jnp.zeros_like(taper))

def resample_tile(tile, shift, frac):
    row_weights = lanczos_matrix(tile.shape[0], shift[0], frac[0])
    col_weights = lanczos_matrix(tile.shape[1], shift[1], frac[1])
    inner = jnp.dot(row_weights, tile, precision=lax.Precision.HIGHEST)
    return jnp.dot(inner, col_weights.T, precision=lax.Precision.HIGHEST)

def coadd_visit(raw, shifts, fracs, segment_ids):
    tiles = raw.reshape(NCCD, TR, TC)

    def warp_one(items):
        return resample_tile(items[0], items[1], items[2])
    warped = lax.map(warp_one, (tiles, shifts, fracs))
    pieces = warped.reshape(NCCD, TR // BR, BR, TC // BC, BC).transpose(0, 1, 3, 2, 4).reshape(NCCD * NB, BR * BC)
    summed = jax.ops.segment_sum(pieces, segment_ids, num_segments=NCCD * NB)
    return summed.reshape(NCCD, TR // BR, TC // BC, BR, BC).transpose(0, 1, 3, 2, 4).reshape(NCCD * TR, TC)

def reference(exposures, lanczos_shift, lanczos_frac, margin_patch, margin_slot):
    segment_ids = (margin_patch[:, :, 0] * NB + margin_slot).reshape(-1).astype(jnp.int32)
    template = coadd_visit(exposures[0], lanczos_shift[0], lanczos_frac[0], segment_ids)
    science = coadd_visit(exposures[1], lanczos_shift[1], lanczos_frac[1], segment_ids)
    reach = KSIDE // 2
    padded_image = jnp.pad(template, reach)
    total_rows = template.shape[0]
    columns = template.shape[1]

    def accumulate(index, carry):
        gram, rhs = carry
        first = (index * BR).astype(jnp.int32)
        window = lax.dynamic_slice(padded_image, (first, jnp.int32(0)), (BR + 2 * reach, columns + 2 * reach))
        stack = jnp.stack([window[r:r + BR, q:q + columns] for r in range(KSIDE) for q in range(KSIDE)]).reshape(KSIDE * KSIDE, BR * columns)
        target = lax.dynamic_slice_in_dim(science, first, BR, 0).reshape(-1)
        gram = gram + jnp.dot(stack, stack.T, precision=lax.Precision.HIGHEST)
        rhs = rhs + jnp.dot(stack, target, precision=lax.Precision.HIGHEST)
        return (gram, rhs)
    start = (jnp.zeros((KB, KB), jnp.float32), jnp.zeros((KB,), jnp.float32))
    gram, rhs = lax.fori_loop(0, total_rows // BR, accumulate, start)
    ridge = 0.001 * jnp.trace(gram) / KB + 1.0
    kernel = jnp.linalg.solve(gram + ridge * jnp.eye(KB, dtype=jnp.float32), rhs)
    model = jnp.zeros_like(science)
    for r in range(KSIDE):
        for q in range(KSIDE):
            model = model + kernel[r * KSIDE + q] * padded_image[r:r + total_rows, q:q + columns]
    return science - model
```

```python
import functools

import jax
import jax.numpy as jnp
import numpy as np
from jax import lax
from jax.experimental import pallas as pl
from jax.experimental.pallas import tpu as pltpu
from jax.sharding import PartitionSpec as P

BR = 32
BC = 128
KSIDE = 5
KB = 25
NB = 32
REACH = KSIDE // 2
SUB = 8
LANES = 128
TAP_LOW, TAP_HIGH = -4, 5
TAPS = tuple(range(TAP_LOW, TAP_HIGH + 1))
LAGS = tuple(range(-(KSIDE - 1), KSIDE))
PRODUCTS = tuple(
    (r2, r, lag)
    for r2 in range(KSIDE)
    for r in range(r2 + 1)
    for lag in (range(KSIDE) if r == r2 else LAGS)
)
MAX_PERMUTES = 32


HIGHEST = lax.Precision.HIGHEST
SMEM = pl.BlockSpec(memory_space=pltpu.SMEM)
VMEM = pl.BlockSpec(memory_space=pltpu.VMEM)


def mm(a, b, contract=((1,), (0,))):
    return lax.dot_general(
        a, b, (contract, ((), ())), precision=HIGHEST, preferred_element_type=jnp.float32
    )


def call(kernel, out_shape, in_specs, scratch, flops, moved, name):
    many = isinstance(out_shape, (list, tuple))
    return pl.pallas_call(
        kernel,
        out_shape=out_shape,
        in_specs=in_specs,
        out_specs=[VMEM] * len(out_shape) if many else VMEM,
        scratch_shapes=scratch,
        cost_estimate=pl.CostEstimate(flops=flops, bytes_accessed=moved, transcendentals=0),
        name=name,
    )


def f32(*shape):
    return jax.ShapeDtypeStruct(shape, jnp.float32)


def lane_ids():
    return lax.broadcasted_iota(jnp.int32, (SUB, LANES), 1)


def shifted(parts, by, lane):
    if by == 0:
        return list(parts)
    turned = [pltpu.roll(part, by % LANES, 1) for part in parts]
    zero = jnp.zeros_like(parts[0])
    out = []
    for j in range(len(parts)):
        beside = j - 1 if by > 0 else j + 1
        other = turned[beside] if 0 <= beside < len(parts) else zero
        keep = lane >= by if by > 0 else lane < LANES + by
        out.append(jnp.where(keep, turned[j], other))
    return out


def sinc(t):
    scaled = jnp.float32(np.pi) * t
    safe = jnp.where(t == 0.0, jnp.float32(1.0), scaled)
    return jnp.where(t == 0.0, jnp.float32(1.0), jnp.sin(safe) / safe)


def tap_weights(shift, frac, lane):
    t = (lane + TAP_LOW).astype(jnp.float32) - shift.astype(jnp.float32) - frac
    w = jnp.where(jnp.abs(t) < 3.0, sinc(t) * sinc(t / 3.0), 0.0)
    return [jnp.broadcast_to(w[:, k : k + 1], (SUB, LANES)) for k in range(len(TAPS))]


def warp_kernel(
    visit, devices, cap, paired, own_ref, tgt_ref, shift_ref, frac_ref, x_ref, *refs
):
    outs, (mid, blocks, inv, cnt) = refs[:-4], refs[-4:]
    rows, columns = x_ref.shape
    slabs, tiles = columns // LANES, rows // SUB
    own = own_ref[0]
    lane = lane_ids()

    @pl.loop(0, devices * cap)
    def _(e):
        inv[e] = 0

    @pl.loop(0, devices)
    def _(p):
        cnt[p] = 0

    @pl.loop(0, NB)
    def _(b):
        p = tgt_ref[own, b]
        c = cnt[p]
        cnt[p] = c + 1
        k = jnp.bitwise_xor(p, own) if paired else p
        inv[k * cap + jnp.minimum(c, cap - 1)] = b

    col_w = tap_weights(shift_ref[visit, 0, 1], frac_ref[visit, 0, 1], lane)
    for j in range(slabs):
        mid[j, 0:SUB, :] = jnp.zeros((SUB, LANES), jnp.float32)
        mid[j, SUB + rows :, :] = jnp.zeros((SUB, LANES), jnp.float32)

    @pl.loop(0, tiles)
    def _(t):
        at = pl.multiple_of(t * SUB, SUB)
        parts = [x_ref[pl.ds(at, SUB), j * LANES : (j + 1) * LANES] for j in range(slabs)]
        total = [jnp.zeros((SUB, LANES), jnp.float32)] * slabs
        for n, d in enumerate(TAPS):
            moved = shifted(parts, -d, lane)
            total = [a + col_w[n] * m for a, m in zip(total, moved)]
        for j in range(slabs):
            mid[j, pl.ds(at + SUB, SUB), :] = total[j]

    row_w = tap_weights(shift_ref[visit, 0, 0], frac_ref[visit, 0, 0], lane)

    @pl.loop(0, slabs)
    def _(j):
        for t in range(tiles):
            first = SUB + t * SUB
            total = jnp.zeros((SUB, LANES), jnp.float32)
            for n, d in enumerate(TAPS):
                total = total + row_w[n] * mid[j, first + d : first + d + SUB, :]
            inner = (t * SUB) % BR
            blocks[(t * SUB) // BR * slabs + j, inner : inner + SUB, :] = total

    if paired:
        for k in range(devices):
            for r in range(cap):
                outs[k][r] = blocks[inv[k * cap + r]]
    else:

        @pl.loop(0, devices * cap)
        def _(e):
            outs[0][e] = blocks[inv[e]]


def sum_blocks(devices, cap, paired, own, table_ref, ins, acc):
    acc[...] = jnp.zeros_like(acc)
    if paired:
        for k in range(devices):
            for r in range(cap):
                slot = table_ref[jnp.bitwise_xor(own, k) * cap + r]
                acc[slot] = acc[slot] + ins[k][r]
    else:

        @pl.loop(0, devices * cap)
        def _(e):
            slot = table_ref[e]
            acc[slot] = acc[slot] + ins[0][e]


def template_kernel(devices, cap, paired, own_ref, table_ref, *refs):
    ins, (out, top, bottom, acc) = refs[:-4], refs[-4:]
    slabs, rows, _ = out.shape
    sum_blocks(devices, cap, paired, own_ref[0], table_ref, ins, acc)
    for s in range(NB):
        out[s % slabs, s // slabs * BR : (s // slabs + 1) * BR, :] = acc[s]
    for j in range(slabs):
        top[j] = acc[j, 0:SUB, :]
        bottom[j] = acc[NB - slabs + j, BR - SUB : BR, :]


def gram_kernel(t_ref, above_ref, below_ref, pick_ref, mask_ref, ext_ref, gram_ref, lagged, gen, spec):
    slabs, rows, _ = t_ref.shape
    lane = lane_ids()
    for j in range(slabs):
        ext_ref[j, 0:SUB, :] = above_ref[j]
        ext_ref[j, SUB : SUB + rows, :] = t_ref[j]
        ext_ref[j, SUB + rows :, :] = below_ref[j]

    @pl.loop(0, rows // SUB + 2)
    def _(t):
        at = pl.ds(pl.multiple_of(t * SUB, SUB), SUB)
        parts = [ext_ref[j, at, :] for j in range(slabs)]
        for n, lag in enumerate(LAGS):
            for j, moved in enumerate(shifted(parts, lag, lane)):
                lagged[n, j, at, :] = moved

    gen[...] = jnp.zeros_like(gen)
    spec[...] = jnp.zeros_like(spec)
    for r2 in range(KSIDE):
        mine = [(n, r, lag) for n, (second, r, lag) in enumerate(PRODUCTS) if second == r2]

        @pl.loop(0, slabs)
        def _(j):
            sums = [None] * len(mine)
            for t in range(rows // SUB):
                base = SUB + t * SUB - REACH
                second = ext_ref[j, base + r2 : base + r2 + SUB, :]
                for m, (_n, r, lag) in enumerate(mine):
                    first = lagged[lag + KSIDE - 1, j, base + r : base + r + SUB, :]
                    term = first * second
                    sums[m] = term if sums[m] is None else sums[m] + term
            edge = ((j == 0) & (lane < REACH)) | ((j == slabs - 1) & (lane >= LANES - REACH))
            for m, (n, _r, _lag) in enumerate(mine):
                gen[n] = gen[n] + jnp.where(edge, 0.0, sums[m])
                spec[n] = spec[n] + jnp.where(edge, sums[m], 0.0)

    src = lax.broadcasted_iota(jnp.int32, (LANES, LANES), 0)
    q2 = lax.rem(lax.broadcasted_iota(jnp.int32, (LANES, LANES), 1), KSIDE)
    late = (src >= REACH) & (q2 - REACH >= src - (LANES - 1))
    inside = jnp.where(((src < REACH) & (q2 - REACH <= src)) | late, 1.0, 0.0)
    data = mm(jnp.sum(gen[...], axis=1), jnp.ones((LANES, LANES), jnp.float32))
    data = data + mm(jnp.sum(spec[...], axis=1), inside)
    total = jnp.zeros(gram_ref.shape, jnp.float32)
    for q in range(KSIDE):
        total = total + mm(pick_ref[q], data * mask_ref[q])
    gram_ref[...] = total


def inverse_kernel(up_ref, full_ref, inv_ref):
    size = up_ref.shape[0]
    up = up_ref[...]
    row = lax.broadcasted_iota(jnp.int32, (size, LANES), 0)
    lane = lax.broadcasted_iota(jnp.int32, (size, LANES), 1)
    square = jnp.concatenate([up, jnp.zeros((LANES - size, LANES), jnp.float32)], axis=0)
    flipped = jnp.transpose(square)[:size]
    diagonal = row == lane
    gram = up + jnp.where(diagonal, 0.0, flipped)
    trace = jnp.sum(jnp.where(diagonal, gram, 0.0), axis=(0, 1), keepdims=True)
    ridge = 0.001 * trace / KB + 1.0
    gram = gram + jnp.where(diagonal & (row < KB), ridge, 0.0)
    full_ref[...] = gram
    work = gram + jnp.where((lane == row + size) & (row < KB), 1.0, 0.0)
    for i in range(KB):
        pivot = work[i : i + 1, :] / work[i : i + 1, i : i + 1]
        work = jnp.where(row == i, pivot, work - work[:, i : i + 1] * pivot)
    inv_ref[...] = jnp.where(lane < KB, pltpu.roll(work, LANES - size, 1), 0.0)


def science_kernel(devices, cap, paired, own_ref, table_ref, ext_ref, *refs):
    ins, (out, rhs_ref, acc, moved, sums_ref) = refs[:-5], refs[-5:]
    slabs, rows, _ = out.shape
    lane = lane_ids()
    sum_blocks(devices, cap, paired, own_ref[0], table_ref, ins, acc)

    for band in range(rows // BR):

        @pl.loop(0, BR // SUB)
        def _(t):
            at = pl.ds(pl.multiple_of(t * SUB, SUB), SUB)
            to = pl.ds(pl.multiple_of(band * BR + t * SUB, SUB), SUB)
            parts = [acc[band * slabs + j, at, :] for j in range(slabs)]
            for j in range(slabs):
                out[j, to, :] = parts[j]
            for q in range(KSIDE):
                for j, part in enumerate(shifted(parts, q - REACH, lane)):
                    moved[q, j, to, :] = part

    def slab(j, sums):
        sums = list(sums)
        for t in range(rows // SUB):
            base = SUB + t * SUB - REACH
            seconds = [moved[q, j, t * SUB : (t + 1) * SUB, :] for q in range(KSIDE)]
            for r in range(KSIDE):
                first = ext_ref[j, base + r : base + r + SUB, :]
                for q in range(KSIDE):
                    sums[r * KSIDE + q] = sums[r * KSIDE + q] + first * seconds[q]
        return tuple(sums)

    sums = lax.fori_loop(0, slabs, slab, (jnp.zeros((SUB, LANES), jnp.float32),) * KB)
    sums_ref[...] = jnp.zeros_like(sums_ref)
    for i in range(KB):
        sums_ref[i : i + 1, :] = jnp.sum(sums[i], axis=0, keepdims=True)
    rhs_ref[...] = mm(
        jnp.ones((SUB, LANES), jnp.float32), sums_ref[...], ((1,), (1,))
    )


def difference_kernel(rhs_ref, full_ref, inv_ref, ext_ref, sci_ref, out_ref, rowed):
    slabs, rows, _ = sci_ref.shape
    size = full_ref.shape[0]
    lane = lane_ids()
    below = jnp.zeros((LANES - size, LANES), jnp.float32)

    def tall(v):
        return jnp.concatenate([v, below], axis=0)

    unit = jnp.where(
        lax.broadcasted_iota(jnp.int32, (size, LANES), 0)
        == lax.broadcasted_iota(jnp.int32, (size, LANES), 1),
        1.0,
        0.0,
    )
    spread = jnp.broadcast_to(rhs_ref[0:1, :], (LANES, LANES))
    rhs = mm(unit, spread, ((1,), (1,)))
    inverse = inv_ref[...]
    kernel = mm(inverse, tall(rhs))
    left = rhs - mm(full_ref[...], tall(kernel))
    kernel = kernel + mm(inverse, tall(left))
    taps = [jnp.broadcast_to(kernel[i : i + 1, :], (SUB, LANES)) for i in range(KB)]

    @pl.loop(0, slabs)
    def _(j):
        for t in range(rows // SUB):
            base = SUB + t * SUB - REACH
            sums = [None] * KSIDE
            for r in range(KSIDE):
                part = ext_ref[j, base + r : base + r + SUB, :]
                for q in range(KSIDE):
                    term = taps[r * KSIDE + q] * part
                    sums[q] = term if sums[q] is None else sums[q] + term
            for q in range(KSIDE):
                rowed[q, j, t * SUB : (t + 1) * SUB, :] = sums[q]

    @pl.loop(0, rows // SUB)
    def _(t):
        at = pl.ds(pl.multiple_of(t * SUB, SUB), SUB)
        total = [jnp.zeros((SUB, LANES), jnp.float32)] * slabs
        for q in range(KSIDE):
            parts = [rowed[q, j, at, :] for j in range(slabs)]
            total = [a + m for a, m in zip(total, shifted(parts, REACH - q, lane))]
        for j in range(slabs):
            out_ref[at, j * LANES : (j + 1) * LANES] = sci_ref[j, at, :] - total[j]


def gram_tables(rows_out):
    count = -(-len(PRODUCTS) // SUB) * SUB
    pick = np.zeros((KSIDE, rows_out, count), np.float32)
    mask = np.zeros((KSIDE, count, LANES), np.float32)
    for n, (r2, r, lag) in enumerate(PRODUCTS):
        for q in range(KSIDE):
            pick[q, r * KSIDE + q, n] = 1.0
            if 0 <= q + lag < KSIDE:
                mask[q, n, r2 * KSIDE + q + lag] = 1.0
    return count, pick, mask


def total_over(value, axis, devices):
    step = 1
    while step < devices:
        pairs = [(i, i ^ step) for i in range(devices)]
        value = value + lax.ppermute(value, axis, pairs)
        step *= 2
    return value


def body(exposures, lanczos_shift, lanczos_frac, margin_patch, margin_slot):
    rows, columns = exposures.shape[1], exposures.shape[2]
    slabs = columns // LANES
    devices = lax.axis_size("ccd")
    owner = lax.axis_index("ccd")
    cap = max(2, 2 * NB // devices)
    paired = devices <= MAX_PERMUTES
    own = owner.astype(jnp.int32).reshape(1)
    targets = margin_patch[:, :, 0]

    chunk = f32(cap, BR, BC)
    packed = [chunk] * devices if paired else [f32(devices * cap, BR, BC)]
    pixels = rows * columns

    def warped(visit):
        out = call(
            functools.partial(warp_kernel, visit, devices, cap, paired),
            packed,
            [SMEM, SMEM, SMEM, SMEM, VMEM],
            [
                pltpu.VMEM((slabs, rows + 2 * SUB, LANES), jnp.float32),
                pltpu.VMEM((NB, BR, BC), jnp.float32),
                pltpu.SMEM((devices * cap,), jnp.int32),
                pltpu.SMEM((devices,), jnp.int32),
            ],
            40 * pixels,
            4 * pixels * 3,
            "warp",
        )(own, targets, lanczos_shift, lanczos_frac, exposures[visit])
        return out

    def exchanged(chunks):
        if not paired:
            return [lax.all_to_all(chunks[0], "ccd", split_axis=0, concat_axis=0, tiled=True)]
        moved = [chunks[0]]
        for k in range(1, devices):
            pairs = [(i, i ^ k) for i in range(devices)]
            moved.append(lax.ppermute(chunks[k], "ccd", pairs))
        return moved

    template_in = exchanged(warped(0))
    science_in = exchanged(warped(1))

    block_ids = jnp.arange(NB)
    earlier = block_ids[None, :] < block_ids[:, None]
    same = targets[:, :, None] == targets[:, None, :]
    order = jnp.sum(same & earlier[None], axis=2)
    arrives = (targets == owner)[:, None, :] & (order[:, None, :] == jnp.arange(cap)[None, :, None])
    table = jnp.where(
        jnp.any(arrives, axis=2), jnp.sum(jnp.where(arrives, margin_slot[:, None, :], 0), axis=2), NB
    ).reshape(-1).astype(jnp.int32)

    slab_shape = f32(slabs, rows, LANES)
    strip = f32(slabs, SUB, LANES)
    sums = pltpu.VMEM((NB + 1, BR, BC), jnp.float32)
    ins = [VMEM] * len(template_in)
    template, top, bottom = call(
        functools.partial(template_kernel, devices, cap, paired),
        [slab_shape, strip, strip],
        [SMEM, SMEM] + ins,
        [sums],
        pixels * 2,
        pixels * 12,
        "template",
    )(own, table, *template_in)
    ends = devices - 1
    above = lax.ppermute(bottom, "ccd", [(i, i + 1) for i in range(ends)])
    below = lax.ppermute(top, "ccd", [(i + 1, i) for i in range(ends)])

    size = NB
    count, pick, mask = gram_tables(size)
    extended, gram = call(
        gram_kernel,
        [f32(slabs, rows + 2 * SUB, LANES), f32(size, LANES)],
        [VMEM] * 5,
        [
            pltpu.VMEM((len(LAGS), slabs, rows + 2 * SUB, LANES), jnp.float32),
            pltpu.VMEM((count, SUB, LANES), jnp.float32),
            pltpu.VMEM((count, SUB, LANES), jnp.float32),
        ],
        pixels * 2 * len(PRODUCTS),
        pixels * 8,
        "gram",
    )(template, above, below, jnp.asarray(pick), jnp.asarray(mask))
    gram = total_over(gram, "ccd", devices)
    full, inverse = call(
        inverse_kernel, [f32(size, LANES)] * 2, [VMEM], [], 10**6, 10**5, "inverse"
    )(gram)

    science, rhs = call(
        functools.partial(science_kernel, devices, cap, paired),
        [slab_shape, f32(SUB, LANES)],
        [SMEM, SMEM, VMEM] + ins,
        [
            sums,
            pltpu.VMEM((KSIDE, slabs, rows, LANES), jnp.float32),
            pltpu.VMEM((LANES, LANES), jnp.float32),
        ],
        pixels * 2 * KB,
        pixels * 16,
        "science",
    )(own, table, extended, *science_in)
    rhs = total_over(rhs, "ccd", devices)

    return call(
        difference_kernel,
        f32(rows, columns),
        [VMEM] * 5,
        [pltpu.VMEM((KSIDE, slabs, rows, LANES), jnp.float32)],
        pixels * 2 * KB,
        pixels * 12,
        "difference",
    )(rhs, full, inverse, extended, science)


def solution(mesh):
    placed = (
        P(None, ("field", "ccd"), None),
        P(None, ("field", "ccd"), None),
        P(None, ("field", "ccd"), None),
        P("field", None, None),
        P("field", None),
    )
    return jax.shard_map(
        body, mesh=mesh, in_specs=placed, out_specs=P(("field", "ccd"), None), check_vma=False
    )
```

```python
import functools

import jax
import jax.numpy as jnp
import numpy as np
from jax import lax
from jax.experimental import pallas as pl
from jax.experimental.pallas import tpu as pltpu
from jax.sharding import PartitionSpec as P


BR = 32
BC = 128
KSIDE = 5
KB = 25
NB = 32
REACH = KSIDE // 2
SUB = 8
LANES = 128
TAP_LOW, TAP_HIGH = -4, 5
TAPS = tuple(range(TAP_LOW, TAP_HIGH + 1))
LAGS = tuple(range(-(KSIDE - 1), KSIDE))
PRODUCTS = tuple(
    (down, lag) for down in range(KSIDE) for lag in (range(KSIDE) if down == 0 else LAGS)
)
EDGE_ROWS = ((0, (0, 1)), (1, (0,)), (-2, (0, 1)), (-1, (0,)))
EDGES = tuple(
    (row, down, lag) for row, downs in EDGE_ROWS for down, lag in PRODUCTS if down in downs
)
MAX_PERMUTES = 32
UNROLL = 4
RHS_LANE = KB


HIGHEST = lax.Precision.HIGHEST
SMEM = pl.BlockSpec(memory_space=pltpu.SMEM)
VMEM = pl.BlockSpec(memory_space=pltpu.VMEM)


def mm(a, b, contract=((1,), (0,))):
    return lax.dot_general(
        a, b, (contract, ((), ())), precision=HIGHEST, preferred_element_type=jnp.float32
    )


def call(kernel, out_shape, in_specs, scratch, flops, moved, grid=()):
    many = isinstance(out_shape, (list, tuple))
    return pl.pallas_call(
        kernel,
        out_shape=out_shape,
        grid=grid,
        in_specs=in_specs,
        out_specs=[VMEM] * len(out_shape) if many else VMEM,
        scratch_shapes=scratch,
        cost_estimate=pl.CostEstimate(flops=flops, bytes_accessed=moved, transcendentals=0),
    )


def f32(*shape):
    return jax.ShapeDtypeStruct(shape, jnp.float32)


def lane_ids():
    return lax.broadcasted_iota(jnp.int32, (SUB, LANES), 1)


def shifted(parts, by, lane):
    if by == 0:
        return list(parts)
    turned = [pltpu.roll(part, by % LANES, 1) for part in parts]
    zero = jnp.zeros_like(parts[0])
    out = []
    for j in range(len(parts)):
        beside = j - 1 if by > 0 else j + 1
        other = turned[beside] if 0 <= beside < len(parts) else zero
        keep = lane >= by if by > 0 else lane < LANES + by
        out.append(jnp.where(keep, turned[j], other))
    return out


def sinc(t):
    scaled = jnp.float32(np.pi) * t
    safe = jnp.where(t == 0.0, jnp.float32(1.0), scaled)
    return jnp.where(t == 0.0, jnp.float32(1.0), jnp.sin(safe) / safe)


def tap_weights(shift, frac, lane):
    t = (lane + TAP_LOW).astype(jnp.float32) - shift.astype(jnp.float32) - frac
    w = jnp.where(jnp.abs(t) < 3.0, sinc(t) * sinc(t / 3.0), 0.0)
    return [jnp.broadcast_to(w[:, k : k + 1], (SUB, LANES)) for k in range(len(TAPS))]


def warp_kernel(
    visit, devices, cap, paired, own_ref, tgt_ref, shift_ref, frac_ref, x_ref, *refs
):
    outs, (mid, blocks, inv, cnt) = refs[:-4], refs[-4:]
    rows, columns = x_ref.shape
    slabs, tiles = columns // LANES, rows // SUB
    own = own_ref[0]
    lane = lane_ids()

    for e in range(devices * cap):
        inv[e] = 0
    for p in range(devices):
        cnt[p] = 0

    def book(b):
        p = tgt_ref[own, b]
        c = cnt[p]
        cnt[p] = c + 1
        k = jnp.bitwise_xor(p, own) if paired else p
        inv[k * cap + jnp.minimum(c, cap - 1)] = b

    col_w = tap_weights(shift_ref[visit, 0, 1], frac_ref[visit, 0, 1], lane)
    row_w = tap_weights(shift_ref[visit, 0, 0], frac_ref[visit, 0, 0], lane)
    for j in range(slabs):
        mid[j, 0:SUB, :] = jnp.zeros((SUB, LANES), jnp.float32)
        mid[j, SUB + rows :, :] = jnp.zeros((SUB, LANES), jnp.float32)

    @pl.loop(0, tiles, unroll=UNROLL)
    def _(t):
        for b in range(NB // tiles):
            book(t * (NB // tiles) + b)
        at = pl.multiple_of(t * SUB, SUB)
        parts = [x_ref[pl.ds(at, SUB), j * LANES : (j + 1) * LANES] for j in range(slabs)]
        total = [jnp.zeros((SUB, LANES), jnp.float32)] * slabs
        for n, d in enumerate(TAPS):
            moved = shifted(parts, -d, lane)
            total = [a + col_w[n] * m for a, m in zip(total, moved)]
        for j in range(slabs):
            mid[j, pl.ds(at + SUB, SUB), :] = total[j]

    @pl.loop(0, slabs)
    def _(j):
        for t in range(tiles):
            first = SUB + t * SUB
            total = jnp.zeros((SUB, LANES), jnp.float32)
            for n, d in enumerate(TAPS):
                total = total + row_w[n] * mid[j, first + d : first + d + SUB, :]
            inner = (t * SUB) % BR
            blocks[(t * SUB) // BR * slabs + j, inner : inner + SUB, :] = total

    if paired:
        for k in range(devices):
            for r in range(cap):
                outs[k][r] = blocks[inv[k * cap + r]]
    else:

        @pl.loop(0, devices * cap)
        def _(e):
            outs[0][e] = blocks[inv[e]]


def sum_blocks(devices, cap, paired, own, table_ref, ins, acc):
    acc[...] = jnp.zeros_like(acc)
    if paired:
        for k in range(devices):
            for r in range(cap):
                slot = table_ref[jnp.bitwise_xor(own, k) * cap + r]
                acc[slot] = acc[slot] + ins[k][r]
    else:

        @pl.loop(0, devices * cap)
        def _(e):
            slot = table_ref[e]
            acc[slot] = acc[slot] + ins[0][e]


def template_kernel(devices, cap, paired, own_ref, table_ref, *refs):
    ins, (out, top, bottom, acc) = refs[:-4], refs[-4:]
    slabs, _, _ = out.shape
    sum_blocks(devices, cap, paired, own_ref[0], table_ref, ins, acc)
    for s in range(NB):
        out[s % slabs, s // slabs * BR : (s // slabs + 1) * BR, :] = acc[s]
    for j in range(slabs):
        top[j] = acc[j, 0:SUB, :]
        bottom[j] = acc[NB - slabs + j, BR - SUB : BR, :]


def gram_kernel(
    ends_ref, t_ref, above_ref, below_ref, coef_ref, ext_ref, gram_ref, lagged, gen, spec
):
    slabs, rows, _ = t_ref.shape
    tiles = rows // SUB
    lane = lane_ids()
    sub = lax.broadcasted_iota(jnp.int32, (SUB, LANES), 0)

    @pl.loop(0, tiles, unroll=UNROLL)
    def _(t):
        at = pl.ds(pl.multiple_of(t * SUB, SUB), SUB)
        parts = [t_ref[j, at, :] for j in range(slabs)]
        for j in range(slabs):
            ext_ref[j, pl.ds(pl.multiple_of(t * SUB + SUB, SUB), SUB), :] = parts[j]
        for n, lag in enumerate(LAGS):
            for j, moved in enumerate(shifted(parts, lag, lane)):
                lagged[n, j, at, :] = moved

    for j in range(slabs):
        ext_ref[j, 0:SUB, :] = above_ref[j]
        ext_ref[j, SUB + rows :, :] = below_ref[j]

    gen[...] = jnp.zeros_like(gen)
    spec[...] = jnp.zeros_like(spec)

    @pl.loop(0, slabs)
    def _(j):
        def firsts(t):
            return [lagged[n, j, t * SUB : (t + 1) * SUB, :] for n in range(len(LAGS))]

        def second(t, down):
            base = SUB + t * SUB + down
            return ext_ref[j, base : base + SUB, :]

        sums = [None] * len(PRODUCTS)
        for t in range(tiles):
            first = firsts(t)
            moved = [second(t, down) for down in range(KSIDE)]
            for n, (down, lag) in enumerate(PRODUCTS):
                term = first[lag + KSIDE - 1] * moved[down]
                sums[n] = term if sums[n] is None else sums[n] + term
        edge = ((j == 0) & (lane < REACH)) | ((j == slabs - 1) & (lane >= LANES - REACH))
        for n in range(len(PRODUCTS)):
            gen[n] = gen[n] + jnp.where(edge, 0.0, sums[n])
            spec[n] = spec[n] + jnp.where(edge, sums[n], 0.0)
        for m, (row, down, lag) in enumerate(EDGES):
            n = len(PRODUCTS) + m
            t = 0 if row >= 0 else tiles - 1
            here = (sub == row % SUB) & (ends_ref[0 if row >= 0 else 1] > 0)
            term = lagged[lag + KSIDE - 1, j, t * SUB : (t + 1) * SUB, :] * second(t, down)
            term = jnp.where(here, term, 0.0)
            gen[n] = gen[n] + jnp.where(edge, 0.0, term)
            spec[n] = spec[n] + jnp.where(edge, term, 0.0)

    src = lax.broadcasted_iota(jnp.int32, (LANES, LANES), 0)
    q2 = lax.rem(lax.broadcasted_iota(jnp.int32, (LANES, LANES), 1), KSIDE)
    late = (src >= REACH) & (q2 - REACH >= src - (LANES - 1))
    inside = jnp.where(((src < REACH) & (q2 - REACH <= src)) | late, 1.0, 0.0)
    data = mm(jnp.sum(gen[...], axis=1), jnp.ones((LANES, LANES), jnp.float32))
    data = data + mm(jnp.sum(spec[...], axis=1), inside)
    gram_ref[...] = jnp.zeros_like(gram_ref)
    for i in range(KB):
        gram_ref[i : i + 1, :] = jnp.sum(coef_ref[i] * data, axis=0, keepdims=True)
    total = gram_ref[...]
    size = total.shape[0]
    below = jnp.zeros((LANES - size, LANES), jnp.float32)
    flipped = jnp.transpose(jnp.concatenate([total, below], axis=0))[:size]
    row = lax.broadcasted_iota(jnp.int32, (size, LANES), 0)
    column = lax.broadcasted_iota(jnp.int32, (size, LANES), 1)
    gram_ref[...] = total + jnp.where(row == column, 0.0, flipped)


def science_kernel(devices, cap, paired, own_ref, table_ref, ext_ref, gram_ref, *refs):
    ins, (out, fit_ref, acc, moved, sums_ref) = refs[:-5], refs[-5:]
    slabs, rows, _ = out.shape
    lane = lane_ids()
    sum_blocks(devices, cap, paired, own_ref[0], table_ref, ins, acc)

    for band in range(rows // BR):

        @pl.loop(0, BR // SUB, unroll=UNROLL)
        def _(t):
            at = pl.ds(pl.multiple_of(t * SUB, SUB), SUB)
            to = pl.ds(pl.multiple_of(band * BR + t * SUB, SUB), SUB)
            parts = [acc[band * slabs + j, at, :] for j in range(slabs)]
            for j in range(slabs):
                out[j, to, :] = parts[j]
            for q in range(KSIDE):
                for j, part in enumerate(shifted(parts, q - REACH, lane)):
                    moved[q, j, to, :] = part

    def slab(j, sums):
        sums = list(sums)
        for t in range(rows // SUB):
            base = SUB + t * SUB - REACH
            seconds = [moved[q, j, t * SUB : (t + 1) * SUB, :] for q in range(KSIDE)]
            for r in range(KSIDE):
                first = ext_ref[j, base + r : base + r + SUB, :]
                for q in range(KSIDE):
                    sums[r * KSIDE + q] = sums[r * KSIDE + q] + first * seconds[q]
        return tuple(sums)

    sums = lax.fori_loop(0, slabs, slab, (jnp.zeros((SUB, LANES), jnp.float32),) * KB)
    sums_ref[...] = jnp.zeros_like(sums_ref)
    for i in range(KB):
        sums_ref[i : i + 1, :] = jnp.sum(sums[i], axis=0, keepdims=True)
    rhs = jnp.sum(sums_ref[...], axis=1, keepdims=True)
    size = gram_ref.shape[0]
    column = lax.broadcasted_iota(jnp.int32, (size, LANES), 1)
    joined = jnp.where(column == RHS_LANE, rhs, gram_ref[...])
    packed = joined[0:SUB]
    for a in range(1, size // SUB):
        packed = packed + pltpu.roll(joined[a * SUB : (a + 1) * SUB], a * size, 1)
    for k in range(devices):
        fit_ref[k] = packed


def solved(packed, size):
    parts = [packed] + [
        pltpu.roll(packed, LANES - a * size, 1) for a in range(1, size // SUB)
    ]
    work = jnp.concatenate(parts, axis=0)
    row = lax.broadcasted_iota(jnp.int32, (size, LANES), 0)
    lane = lax.broadcasted_iota(jnp.int32, (size, LANES), 1)
    diagonal = (row == lane) & (row < KB)
    trace = jnp.sum(jnp.where(diagonal, work, 0.0), axis=(0, 1), keepdims=True)
    ridge = 0.001 * trace / KB + 1.0
    work = jnp.where(lane < size, jnp.where(diagonal, work + ridge, work), 0.0)
    for i in range(KB):
        pivot = work[i : i + 1, :] / work[i : i + 1, i : i + 1]
        work = jnp.where(row == i, pivot, work - work[:, i : i + 1] * pivot)
    return work[:, RHS_LANE : RHS_LANE + 1]


def difference_kernel(fit_ref, ext_ref, sci_ref, out_ref, rowed):
    slabs, rows, _ = sci_ref.shape
    lane = lane_ids()
    shared = fit_ref[0]
    for k in range(1, fit_ref.shape[0]):
        shared = shared + fit_ref[k]
    kernel = solved(shared, NB)
    taps = [jnp.broadcast_to(kernel[i : i + 1, :], (SUB, LANES)) for i in range(KB)]

    @pl.loop(0, slabs)
    def _(j):
        for t in range(rows // SUB):
            base = SUB + t * SUB - REACH
            sums = [None] * KSIDE
            for r in range(KSIDE):
                part = ext_ref[j, base + r : base + r + SUB, :]
                for q in range(KSIDE):
                    term = taps[r * KSIDE + q] * part
                    sums[q] = term if sums[q] is None else sums[q] + term
            for q in range(KSIDE):
                rowed[q, j, t * SUB : (t + 1) * SUB, :] = sums[q]

    @pl.loop(0, rows // SUB, unroll=UNROLL)
    def _(t):
        at = pl.ds(pl.multiple_of(t * SUB, SUB), SUB)
        total = [jnp.zeros((SUB, LANES), jnp.float32)] * slabs
        for q in range(KSIDE):
            parts = [rowed[q, j, at, :] for j in range(slabs)]
            total = [a + m for a, m in zip(total, shifted(parts, REACH - q, lane))]
        for j in range(slabs):
            out_ref[at, j * LANES : (j + 1) * LANES] = sci_ref[j, at, :] - total[j]


def by_permutes(devices):
    return devices <= MAX_PERMUTES and devices & (devices - 1) == 0


def gram_table():
    count = -(-(len(PRODUCTS) + len(EDGES)) // SUB) * SUB
    coef = np.zeros((KB, count, LANES), np.float32)
    left_out = {0: (-2, -1), 1: (-1,), 2: (), 3: (0,), 4: (0, 1)}
    for r in range(KSIDE):
        for q in range(KSIDE):
            for n, (row, down, lag) in enumerate([(None, *p) for p in PRODUCTS] + list(EDGES)):
                if r + down < KSIDE and 0 <= q + lag < KSIDE:
                    column = (r + down) * KSIDE + q + lag
                    if row is None:
                        coef[r * KSIDE + q, n, column] = 1.0
                    elif row in left_out[r]:
                        coef[r * KSIDE + q, n, column] = -1.0
    return count, coef


def body(exposures, lanczos_shift, lanczos_frac, margin_patch, margin_slot):
    rows, columns = exposures.shape[1], exposures.shape[2]
    slabs = columns // LANES
    devices = lax.axis_size("ccd")
    owner = lax.axis_index("ccd")
    cap = max(2, 2 * NB // devices)
    paired = by_permutes(devices)
    own = owner.astype(jnp.int32).reshape(1)
    targets = margin_patch[:, :, 0]

    pixels = rows * columns

    def warped(visit, paired):
        out = call(
            functools.partial(warp_kernel, visit, devices, cap, paired),
            [f32(cap, BR, BC)] * devices if paired else [f32(devices * cap, BR, BC)],
            [SMEM, SMEM, SMEM, SMEM, pl.BlockSpec((None, rows, columns), lambda i: (visit, 0, 0))],
            [
                pltpu.VMEM((slabs, rows + 2 * SUB, LANES), jnp.float32),
                pltpu.VMEM((NB, BR, BC), jnp.float32),
                pltpu.SMEM((devices * cap,), jnp.int32),
                pltpu.SMEM((devices,), jnp.int32),
            ],
            40 * pixels,
            4 * pixels * 3,
            (1,),
        )(own, targets, lanczos_shift, lanczos_frac, exposures)
        return out

    def exchanged(chunks):
        if len(chunks) == 1:
            return [lax.all_to_all(chunks[0], "ccd", split_axis=0, concat_axis=0, tiled=True)]
        moved = [chunks[0]]
        for k in range(1, devices):
            moved.append(
                lax.ppermute(chunks[k], "ccd", [(i, i ^ k) for i in range(devices)])
            )
        return moved

    template_chunks = warped(0, False)
    science_chunks = warped(1, paired)
    template_in = exchanged(template_chunks)
    science_in = exchanged(science_chunks)

    block_ids = jnp.arange(NB)
    earlier = block_ids[None, :] < block_ids[:, None]
    same = targets[:, :, None] == targets[:, None, :]
    order = jnp.sum(same & earlier[None], axis=2)
    arrives = (targets == owner)[:, None, :] & (order[:, None, :] == jnp.arange(cap)[None, :, None])
    table = jnp.where(
        jnp.any(arrives, axis=2), jnp.sum(jnp.where(arrives, margin_slot[:, None, :], 0), axis=2), NB
    ).reshape(-1).astype(jnp.int32)

    slab_shape = f32(slabs, rows, LANES)
    strip = f32(slabs, SUB, LANES)
    sums = pltpu.VMEM((NB + 1, BR, BC), jnp.float32)
    template, top, bottom = call(
        functools.partial(template_kernel, devices, cap, False),
        [slab_shape, strip, strip],
        [SMEM, SMEM, VMEM],
        [sums],
        pixels * 2,
        pixels * 12,
    )(own, table, *template_in)
    ends = devices - 1
    above = lax.ppermute(bottom, "ccd", [(i, i + 1) for i in range(ends)])
    below = lax.ppermute(top, "ccd", [(i + 1, i) for i in range(ends)])

    size = NB
    count, coef = gram_table()
    at_ends = jnp.stack([owner == 0, owner == devices - 1]).astype(jnp.int32)
    extended, gram = call(
        gram_kernel,
        [f32(slabs, rows + 2 * SUB, LANES), f32(size, LANES)],
        [SMEM] + [VMEM] * 4,
        [
            pltpu.VMEM((len(LAGS), slabs, rows, LANES), jnp.float32),
            pltpu.VMEM((count, SUB, LANES), jnp.float32),
            pltpu.VMEM((count, SUB, LANES), jnp.float32),
        ],
        pixels * 2 * len(PRODUCTS),
        pixels * 8,
    )(at_ends, template, above, below, jnp.asarray(coef))

    science, fit = call(
        functools.partial(science_kernel, devices, cap, paired),
        [slab_shape, f32(devices, SUB, LANES)],
        [SMEM, SMEM, VMEM, VMEM] + [VMEM] * len(science_in),
        [
            sums,
            pltpu.VMEM((KSIDE, slabs, rows, LANES), jnp.float32),
            pltpu.VMEM((size, LANES), jnp.float32),
        ],
        pixels * 2 * KB,
        pixels * 16,
    )(own, table, extended, gram, *science_in)
    fit = lax.all_to_all(fit, "ccd", split_axis=0, concat_axis=0, tiled=True)

    return call(
        difference_kernel,
        f32(rows, columns),
        [VMEM] * 3,
        [pltpu.VMEM((KSIDE, slabs, rows, LANES), jnp.float32)],
        pixels * 2 * KB,
        pixels * 12,
    )(fit, extended, science)


def solution(mesh):
    placed = (
        P(None, ("field", "ccd"), None),
        P(None, ("field", "ccd"), None),
        P(None, ("field", "ccd"), None),
        P("field", None, None),
        P("field", None),
    )
    return jax.shard_map(
        body, mesh=mesh, in_specs=placed, out_specs=P(("field", "ccd"), None), check_vma=False
    )
```

```python
import functools

import jax
import jax.numpy as jnp
import numpy as np
from jax import lax
from jax.experimental import pallas as pl
from jax.experimental.pallas import tpu as pltpu
from jax.sharding import PartitionSpec as P


BR = 32
BC = 128
KSIDE = 5
KB = 25
NB = 32
REACH = KSIDE // 2
SUB = 8
LANES = 128
TAP_LOW, TAP_HIGH = -4, 5
TAPS = tuple(range(TAP_LOW, TAP_HIGH + 1))
LAGS = tuple(range(-(KSIDE - 1), KSIDE))
PRODUCTS = tuple(
    (down, lag) for down in range(KSIDE) for lag in (range(KSIDE) if down == 0 else LAGS)
)
EDGE_ROWS = ((0, (0, 1)), (1, (0,)), (-2, (0, 1)), (-1, (0,)))
EDGES = tuple(
    (row, down, lag) for row, downs in EDGE_ROWS for down, lag in PRODUCTS if down in downs
)
MAX_PERMUTES = 32
UNROLL = 4
RHS_LANE = KB


HIGHEST = lax.Precision.HIGHEST
SMEM = pl.BlockSpec(memory_space=pltpu.SMEM)
VMEM = pl.BlockSpec(memory_space=pltpu.VMEM)


def mm(a, b, contract=((1,), (0,))):
    return lax.dot_general(
        a, b, (contract, ((), ())), precision=HIGHEST, preferred_element_type=jnp.float32
    )


def call(kernel, out_shape, in_specs, scratch, flops, moved, grid=()):
    many = isinstance(out_shape, (list, tuple))
    return pl.pallas_call(
        kernel,
        out_shape=out_shape,
        grid=grid,
        in_specs=in_specs,
        out_specs=[VMEM] * len(out_shape) if many else VMEM,
        scratch_shapes=scratch,
        cost_estimate=pl.CostEstimate(flops=flops, bytes_accessed=moved, transcendentals=0),
    )


def f32(*shape):
    return jax.ShapeDtypeStruct(shape, jnp.float32)


def lane_ids():
    return lax.broadcasted_iota(jnp.int32, (SUB, LANES), 1)


def shifted(parts, by, lane):
    if by == 0:
        return list(parts)
    turned = [pltpu.roll(part, by % LANES, 1) for part in parts]
    zero = jnp.zeros_like(parts[0])
    out = []
    for j in range(len(parts)):
        beside = j - 1 if by > 0 else j + 1
        other = turned[beside] if 0 <= beside < len(parts) else zero
        keep = lane >= by if by > 0 else lane < LANES + by
        out.append(jnp.where(keep, turned[j], other))
    return out


def sinc(t):
    scaled = jnp.float32(np.pi) * t
    safe = jnp.where(t == 0.0, jnp.float32(1.0), scaled)
    return jnp.where(t == 0.0, jnp.float32(1.0), jnp.sin(safe) / safe)


def tap_weights(shift, frac, lane):
    t = (lane + TAP_LOW).astype(jnp.float32) - shift.astype(jnp.float32) - frac
    w = jnp.where(jnp.abs(t) < 3.0, sinc(t) * sinc(t / 3.0), 0.0)
    return [jnp.broadcast_to(w[:, k : k + 1], (SUB, LANES)) for k in range(len(TAPS))]


def warp_kernel(
    visit, devices, cap, paired, strips, own_ref, tgt_ref, shift_ref, frac_ref, x_ref, *refs
):
    outs, (mid, blocks, inv, cnt) = refs[:-4], refs[-4:]
    rows, columns = x_ref.shape
    slabs, tiles = columns // LANES, rows // SUB
    own = own_ref[0]
    lane = lane_ids()

    for e in range(devices * cap):
        inv[e] = 0
    for p in range(devices):
        cnt[p] = 0

    def book(b):
        p = tgt_ref[own, b]
        c = cnt[p]
        cnt[p] = c + 1
        k = jnp.bitwise_xor(p, own) if paired else p
        inv[k * cap + jnp.minimum(c, cap - 1)] = b

    col_w = tap_weights(shift_ref[visit, 0, 1], frac_ref[visit, 0, 1], lane)
    row_w = tap_weights(shift_ref[visit, 0, 0], frac_ref[visit, 0, 0], lane)
    for j in range(slabs):
        mid[j, 0:SUB, :] = jnp.zeros((SUB, LANES), jnp.float32)
        mid[j, SUB + rows :, :] = jnp.zeros((SUB, LANES), jnp.float32)

    @pl.loop(0, tiles, unroll=UNROLL)
    def _(t):
        for b in range(NB // tiles):
            book(t * (NB // tiles) + b)
        at = pl.multiple_of(t * SUB, SUB)
        parts = [x_ref[pl.ds(at, SUB), j * LANES : (j + 1) * LANES] for j in range(slabs)]
        total = [jnp.zeros((SUB, LANES), jnp.float32)] * slabs
        for n, d in enumerate(TAPS):
            moved = shifted(parts, -d, lane)
            total = [a + col_w[n] * m for a, m in zip(total, moved)]
        for j in range(slabs):
            mid[j, pl.ds(at + SUB, SUB), :] = total[j]

    @pl.loop(0, slabs)
    def _(j):
        for t in range(tiles):
            first = SUB + t * SUB
            total = jnp.zeros((SUB, LANES), jnp.float32)
            for n, d in enumerate(TAPS):
                total = total + row_w[n] * mid[j, first + d : first + d + SUB, :]
            inner = (t * SUB) % BR
            blocks[(t * SUB) // BR * slabs + j, inner : inner + SUB, :] = total

    if paired:
        for k in range(devices):
            for r in range(cap):
                outs[k][r] = blocks[inv[k * cap + r]]
    else:

        @pl.loop(0, devices)
        def _(p):
            for r in range(cap):
                outs[0][p, r * BR : (r + 1) * BR, :] = blocks[inv[p * cap + r]]
            if strips:
                before = jnp.maximum(p - 1, 0)
                after = jnp.minimum(p + 1, devices - 1)
                outs[0][p, cap * BR :, :] = jnp.zeros((2 * SUB, LANES), jnp.float32)
                for r in range(cap):
                    at = cap * BR + REACH * r
                    outs[0][p, at : at + REACH, :] = blocks[
                        inv[before * cap + r], BR - REACH : BR, :
                    ]
                    at = at + SUB
                    outs[0][p, at : at + REACH, :] = blocks[inv[after * cap + r], 0:REACH, :]


def sum_blocks(devices, cap, paired, own, table_ref, ins, acc):
    acc[...] = jnp.zeros_like(acc)
    if paired:
        for k in range(devices):
            for r in range(cap):
                slot = table_ref[jnp.bitwise_xor(own, k) * cap + r]
                acc[slot] = acc[slot] + ins[k][r]
    else:

        @pl.loop(0, devices)
        def _(c):
            for r in range(cap):
                slot = table_ref[c * cap + r]
                acc[slot] = acc[slot] + ins[0][c, r * BR : (r + 1) * BR, :]


def template_kernel(
    devices, cap, own_ref, table_ref, ends_ref, in_ref, edges_ref, coef_ref,
    ext_ref, gram_ref, acc, lagged, gen, spec,
):
    slabs, rows = ext_ref.shape[0], ext_ref.shape[1] - 2 * SUB
    tiles = rows // SUB
    lane = lane_ids()
    sub = lax.broadcasted_iota(jnp.int32, (SUB, LANES), 0)
    sum_blocks(devices, cap, False, own_ref[0], table_ref, [in_ref], acc)

    for end in range(2):
        at = cap * BR + end * SUB
        strip = in_ref[:, at : at + SUB, :].reshape(devices * SUB, LANES)
        edge = mm(edges_ref[end], strip)
        first = SUB - REACH if end == 0 else SUB + rows
        for j in range(slabs):
            whole = 0 if end == 0 else SUB + rows
            ext_ref[j, whole : whole + SUB, :] = jnp.zeros((SUB, LANES), jnp.float32)
            for i in range(REACH):
                ext_ref[j, first + i : first + i + 1, :] = edge[i * slabs + j : i * slabs + j + 1]

    def lag_tile(parts, at):
        for n, lag in enumerate(LAGS):
            for j, moved in enumerate(shifted(parts, lag, lane)):
                lagged[n, j, at, :] = moved

    lag_tile([ext_ref[j, 0:SUB, :] for j in range(slabs)], slice(0, SUB))
    for band in range(rows // BR):

        @pl.loop(0, BR // SUB, unroll=UNROLL)
        def _(t):
            at = pl.ds(pl.multiple_of(t * SUB, SUB), SUB)
            to = pl.ds(pl.multiple_of(SUB + band * BR + t * SUB, SUB), SUB)
            parts = [acc[band * slabs + j, at, :] for j in range(slabs)]
            for j in range(slabs):
                ext_ref[j, to, :] = parts[j]
            lag_tile(parts, to)

    gen[...] = jnp.zeros_like(gen)
    spec[...] = jnp.zeros_like(spec)

    @pl.loop(0, slabs)
    def _(j):
        def first(t, down, lag):
            base = SUB + t * SUB - down // 2
            return lagged[lag + KSIDE - 1, j, base : base + SUB, :]

        def second(t, down):
            base = SUB + t * SUB + down
            return ext_ref[j, base : base + SUB, :]

        sums = [None] * len(PRODUCTS)
        for t in range(tiles):
            moved = [second(t, down - down // 2) for down in range(KSIDE)]
            for n, (down, lag) in enumerate(PRODUCTS):
                term = first(t, down, lag) * moved[down]
                sums[n] = term if sums[n] is None else sums[n] + term
        edge = ((j == 0) & (lane < REACH)) | ((j == slabs - 1) & (lane >= LANES - REACH))
        for n in range(len(PRODUCTS)):
            gen[n] = gen[n] + jnp.where(edge, 0.0, sums[n])
            spec[n] = spec[n] + jnp.where(edge, sums[n], 0.0)
        for m, (row, down, lag) in enumerate(EDGES):
            n = len(PRODUCTS) + m
            t = 0 if row >= 0 else tiles - 1
            here = (sub == row % SUB) & (ends_ref[0 if row >= 0 else 1] > 0)
            term = first(t, 0, lag) * second(t, down)
            term = jnp.where(here, term, 0.0)
            gen[n] = gen[n] + jnp.where(edge, 0.0, term)
            spec[n] = spec[n] + jnp.where(edge, term, 0.0)

    src = lax.broadcasted_iota(jnp.int32, (LANES, LANES), 0)
    q2 = lax.rem(lax.broadcasted_iota(jnp.int32, (LANES, LANES), 1), KSIDE)
    late = (src >= REACH) & (q2 - REACH >= src - (LANES - 1))
    inside = jnp.where(((src < REACH) & (q2 - REACH <= src)) | late, 1.0, 0.0)
    data = mm(jnp.sum(gen[...], axis=1), jnp.ones((LANES, LANES), jnp.float32))
    data = data + mm(jnp.sum(spec[...], axis=1), inside)
    gram_ref[...] = jnp.zeros_like(gram_ref)
    for i in range(KB):
        gram_ref[i : i + 1, :] = jnp.sum(coef_ref[i] * data, axis=0, keepdims=True)
    total = gram_ref[...]
    size = total.shape[0]
    below = jnp.zeros((LANES - size, LANES), jnp.float32)
    flipped = jnp.transpose(jnp.concatenate([total, below], axis=0))[:size]
    row = lax.broadcasted_iota(jnp.int32, (size, LANES), 0)
    column = lax.broadcasted_iota(jnp.int32, (size, LANES), 1)
    gram_ref[...] = total + jnp.where(row == column, 0.0, flipped)


def science_kernel(devices, cap, paired, own_ref, table_ref, ext_ref, gram_ref, *refs):
    ins, (out, fit_ref, acc, moved, sums_ref) = refs[:-5], refs[-5:]
    slabs, rows, _ = out.shape
    lane = lane_ids()
    sum_blocks(devices, cap, paired, own_ref[0], table_ref, ins, acc)

    for band in range(rows // BR):

        @pl.loop(0, BR // SUB, unroll=UNROLL)
        def _(t):
            at = pl.ds(pl.multiple_of(t * SUB, SUB), SUB)
            to = pl.ds(pl.multiple_of(band * BR + t * SUB, SUB), SUB)
            parts = [acc[band * slabs + j, at, :] for j in range(slabs)]
            for j in range(slabs):
                out[j, to, :] = parts[j]
            for q in range(KSIDE):
                for j, part in enumerate(shifted(parts, q - REACH, lane)):
                    moved[q, j, to, :] = part

    def slab(j, sums):
        sums = list(sums)
        for t in range(rows // SUB):
            base = SUB + t * SUB - REACH
            seconds = [moved[q, j, t * SUB : (t + 1) * SUB, :] for q in range(KSIDE)]
            for r in range(KSIDE):
                first = ext_ref[j, base + r : base + r + SUB, :]
                for q in range(KSIDE):
                    sums[r * KSIDE + q] = sums[r * KSIDE + q] + first * seconds[q]
        return tuple(sums)

    sums = lax.fori_loop(0, slabs, slab, (jnp.zeros((SUB, LANES), jnp.float32),) * KB)
    sums_ref[...] = jnp.zeros_like(sums_ref)
    for i in range(KB):
        sums_ref[i : i + 1, :] = jnp.sum(sums[i], axis=0, keepdims=True)
    rhs = jnp.sum(sums_ref[...], axis=1, keepdims=True)
    size = gram_ref.shape[0]
    column = lax.broadcasted_iota(jnp.int32, (size, LANES), 1)
    joined = jnp.where(column == RHS_LANE, rhs, gram_ref[...])
    packed = joined[0:SUB]
    for a in range(1, size // SUB):
        packed = packed + pltpu.roll(joined[a * SUB : (a + 1) * SUB], a * size, 1)
    for k in range(devices):
        fit_ref[k] = packed


def solved(packed, size):
    parts = [packed] + [
        pltpu.roll(packed, LANES - a * size, 1) for a in range(1, size // SUB)
    ]
    work = jnp.concatenate(parts, axis=0)
    row = lax.broadcasted_iota(jnp.int32, (size, LANES), 0)
    lane = lax.broadcasted_iota(jnp.int32, (size, LANES), 1)
    diagonal = (row == lane) & (row < KB)
    trace = jnp.sum(jnp.where(diagonal, work, 0.0), axis=(0, 1), keepdims=True)
    ridge = 0.001 * trace / KB + 1.0
    work = jnp.where(lane < size, jnp.where(diagonal, work + ridge, work), 0.0)
    for i in range(KB):
        pivot = work[i : i + 1, :] / work[i : i + 1, i : i + 1]
        work = jnp.where(row == i, pivot, work - work[:, i : i + 1] * pivot)
    return work[:, RHS_LANE : RHS_LANE + 1]


def difference_kernel(fit_ref, ext_ref, sci_ref, out_ref, rowed):
    slabs, rows, _ = sci_ref.shape
    lane = lane_ids()
    shared = fit_ref[0]
    for k in range(1, fit_ref.shape[0]):
        shared = shared + fit_ref[k]
    kernel = solved(shared, NB)
    taps = [jnp.broadcast_to(kernel[i : i + 1, :], (SUB, LANES)) for i in range(KB)]

    @pl.loop(0, slabs)
    def _(j):
        for t in range(rows // SUB):
            base = SUB + t * SUB - REACH
            sums = [None] * KSIDE
            for r in range(KSIDE):
                part = ext_ref[j, base + r : base + r + SUB, :]
                for q in range(KSIDE):
                    term = taps[r * KSIDE + q] * part
                    sums[q] = term if sums[q] is None else sums[q] + term
            for q in range(KSIDE):
                rowed[q, j, t * SUB : (t + 1) * SUB, :] = sums[q]

    @pl.loop(0, rows // SUB, unroll=UNROLL)
    def _(t):
        at = pl.ds(pl.multiple_of(t * SUB, SUB), SUB)
        total = [jnp.zeros((SUB, LANES), jnp.float32)] * slabs
        for q in range(KSIDE):
            parts = [rowed[q, j, at, :] for j in range(slabs)]
            total = [a + m for a, m in zip(total, shifted(parts, REACH - q, lane))]
        for j in range(slabs):
            out_ref[at, j * LANES : (j + 1) * LANES] = sci_ref[j, at, :] - total[j]


def by_permutes(devices):
    return devices <= MAX_PERMUTES and devices & (devices - 1) == 0


def gram_table():
    count = -(-(len(PRODUCTS) + len(EDGES)) // SUB) * SUB
    coef = np.zeros((KB, count, LANES), np.float32)
    left_out = {0: (-2, -1), 1: (-1,), 2: (), 3: (0,), 4: (0, 1)}
    for r in range(KSIDE):
        for q in range(KSIDE):
            for n, (row, down, lag) in enumerate([(None, *p) for p in PRODUCTS] + list(EDGES)):
                if r + down < KSIDE and 0 <= q + lag < KSIDE:
                    column = (r + down) * KSIDE + q + lag
                    if row is None:
                        coef[r * KSIDE + q, n, column] = 1.0
                    elif row in left_out[r]:
                        coef[r * KSIDE + q, n, column] = -1.0
    return count, coef


def body(exposures, lanczos_shift, lanczos_frac, margin_patch, margin_slot):
    rows, columns = exposures.shape[1], exposures.shape[2]
    slabs = columns // LANES
    devices = lax.axis_size("ccd")
    owner = lax.axis_index("ccd")
    cap = max(2, 2 * NB // devices)
    paired = by_permutes(devices)
    own = owner.astype(jnp.int32).reshape(1)
    targets = margin_patch[:, :, 0]

    pixels = rows * columns

    def warped(visit, paired):
        out = call(
            functools.partial(warp_kernel, visit, devices, cap, paired, visit == 0),
            [f32(cap, BR, BC)] * devices
            if paired
            else [f32(devices, cap * BR + (2 * SUB if visit == 0 else 0), BC)],
            [SMEM, SMEM, SMEM, SMEM, pl.BlockSpec((None, rows, columns), lambda i: (visit, 0, 0))],
            [
                pltpu.VMEM((slabs, rows + 2 * SUB, LANES), jnp.float32),
                pltpu.VMEM((NB, BR, BC), jnp.float32),
                pltpu.SMEM((devices * cap,), jnp.int32),
                pltpu.SMEM((devices,), jnp.int32),
            ],
            40 * pixels,
            4 * pixels * 3,
            (1,),
        )(own, targets, lanczos_shift, lanczos_frac, exposures)
        return out

    def exchanged(chunks):
        if len(chunks) == 1:
            return [lax.all_to_all(chunks[0], "ccd", split_axis=0, concat_axis=0, tiled=True)]
        moved = [chunks[0]]
        for k in range(1, devices):
            moved.append(
                lax.ppermute(chunks[k], "ccd", [(i, i ^ k) for i in range(devices)])
            )
        return moved

    template_chunks = warped(0, False)
    science_chunks = warped(1, paired)
    template_in = exchanged(template_chunks)
    science_in = exchanged(science_chunks)

    block_ids = jnp.arange(NB)
    earlier = block_ids[None, :] < block_ids[:, None]
    same = targets[:, :, None] == targets[:, None, :]
    order = jnp.sum(same & earlier[None], axis=2)
    in_place = order[:, None, :] == jnp.arange(cap)[None, :, None]

    def slots_at(patch):
        arrives = (targets == patch)[:, None, :] & in_place
        slots = jnp.sum(jnp.where(arrives, margin_slot[:, None, :], 0), axis=2)
        return jnp.where(jnp.any(arrives, axis=2), slots, NB).astype(jnp.int32)

    table = slots_at(owner).reshape(-1)
    wanted = jnp.arange(REACH * slabs)[:, None, None, None]
    row_of = jnp.arange(SUB // REACH * REACH).reshape(1, 1, SUB // REACH, REACH) % REACH
    spare = ((0, 0), (0, SUB // REACH - cap))

    def edge_rows(patch, first_slot):
        slots = jnp.pad(slots_at(patch), spare, constant_values=NB)[None, :, :, None]
        hit = (slots - first_slot == wanted % slabs) & (row_of == wanted // slabs)
        return hit.astype(jnp.float32).reshape(REACH * slabs, devices * SUB)

    edges = jnp.stack([edge_rows(owner - 1, NB - slabs), edge_rows(owner + 1, 0)])

    slab_shape = f32(slabs, rows, LANES)
    sums = pltpu.VMEM((NB + 1, BR, BC), jnp.float32)
    size = NB
    count, coef = gram_table()
    at_ends = jnp.stack([owner == 0, owner == devices - 1]).astype(jnp.int32)
    extended, gram = call(
        functools.partial(template_kernel, devices, cap),
        [f32(slabs, rows + 2 * SUB, LANES), f32(size, LANES)],
        [SMEM, SMEM, SMEM] + [VMEM] * 3,
        [
            sums,
            pltpu.VMEM((len(LAGS), slabs, rows + SUB, LANES), jnp.float32),
            pltpu.VMEM((count, SUB, LANES), jnp.float32),
            pltpu.VMEM((count, SUB, LANES), jnp.float32),
        ],
        pixels * 2 * len(PRODUCTS),
        pixels * 8,
    )(own, table, at_ends, template_in[0], edges, jnp.asarray(coef))

    science, fit = call(
        functools.partial(science_kernel, devices, cap, paired),
        [slab_shape, f32(devices, SUB, LANES)],
        [SMEM, SMEM, VMEM, VMEM] + [VMEM] * len(science_in),
        [
            sums,
            pltpu.VMEM((KSIDE, slabs, rows, LANES), jnp.float32),
            pltpu.VMEM((size, LANES), jnp.float32),
        ],
        pixels * 2 * KB,
        pixels * 16,
    )(own, table, extended, gram, *science_in)
    fit = lax.all_to_all(fit, "ccd", split_axis=0, concat_axis=0, tiled=True)

    return call(
        difference_kernel,
        f32(rows, columns),
        [VMEM] * 3,
        [pltpu.VMEM((KSIDE, slabs, rows, LANES), jnp.float32)],
        pixels * 2 * KB,
        pixels * 12,
    )(fit, extended, science)


def solution(mesh):
    placed = (
        P(None, ("field", "ccd"), None),
        P(None, ("field", "ccd"), None),
        P(None, ("field", "ccd"), None),
        P("field", None, None),
        P("field", None),
    )
    return jax.shard_map(
        body, mesh=mesh, in_specs=placed, out_specs=P(("field", "ccd"), None), check_vma=False
    )
```

```python
import functools

import jax
import jax.numpy as jnp
import numpy as np
from jax import lax
from jax.experimental import pallas as pl
from jax.experimental.pallas import tpu as pltpu
from jax.sharding import PartitionSpec as P


BR = 32
BC = 128
KSIDE = 5
KB = 25
NB = 32
REACH = KSIDE // 2
SUB = 8
LANES = 128
TAP_LOW, TAP_HIGH = -4, 5
TAPS = tuple(range(TAP_LOW, TAP_HIGH + 1))
LAGS = tuple(range(-(KSIDE - 1), KSIDE))
PRODUCTS = tuple(
    (down, lag) for down in range(KSIDE) for lag in (range(KSIDE) if down == 0 else LAGS)
)
EDGE_ROWS = ((0, (0, 1)), (1, (0,)), (-2, (0, 1)), (-1, (0,)))
EDGES = tuple(
    (row, down, lag) for row, downs in EDGE_ROWS for down, lag in PRODUCTS if down in downs
)
MAX_PERMUTES = 32
UNROLL = 4
STEP = 4
GROUP = 5
RHS_LANE = KB


HIGHEST = lax.Precision.HIGHEST
SMEM = pl.BlockSpec(memory_space=pltpu.SMEM)
VMEM = pl.BlockSpec(memory_space=pltpu.VMEM)


def mm(a, b, contract=((1,), (0,))):
    return lax.dot_general(
        a, b, (contract, ((), ())), precision=HIGHEST, preferred_element_type=jnp.float32
    )


def call(kernel, out_shape, in_specs, scratch, flops, moved, grid=(), room=16, out=VMEM):
    many = isinstance(out_shape, (list, tuple))
    return pl.pallas_call(
        kernel,
        out_shape=out_shape,
        grid=grid,
        in_specs=in_specs,
        out_specs=[out] * len(out_shape) if many else out,
        scratch_shapes=scratch,
        cost_estimate=pl.CostEstimate(flops=flops, bytes_accessed=moved, transcendentals=0),
        compiler_params=pltpu.CompilerParams(vmem_limit_bytes=room << 20 if room else None),
    )


def f32(*shape):
    return jax.ShapeDtypeStruct(shape, jnp.float32)


def lane_ids():
    return lax.broadcasted_iota(jnp.int32, (SUB, LANES), 1)


def shifted(parts, by, lane):
    if by == 0:
        return list(parts)
    turned = [pltpu.roll(part, by % LANES, 1) for part in parts]
    zero = jnp.zeros_like(parts[0])
    out = []
    for j in range(len(parts)):
        beside = j - 1 if by > 0 else j + 1
        other = turned[beside] if 0 <= beside < len(parts) else zero
        keep = lane >= by if by > 0 else lane < LANES + by
        out.append(jnp.where(keep, turned[j], other))
    return out


def sinc(t):
    scaled = jnp.float32(np.pi) * t
    safe = jnp.where(t == 0.0, jnp.float32(1.0), scaled)
    return jnp.where(t == 0.0, jnp.float32(1.0), jnp.sin(safe) / safe)


def tap_weights(shift, frac, lane):
    t = (lane + TAP_LOW).astype(jnp.float32) - shift.astype(jnp.float32) - frac
    w = jnp.where(jnp.abs(t) < 3.0, sinc(t) * sinc(t / 3.0), 0.0)
    return [jnp.broadcast_to(w[:, k : k + 1], (SUB, LANES)) for k in range(len(TAPS))]


def warp_kernel(
    visit, devices, cap, paired, own_ref, tgt_ref, shift_ref, frac_ref, x_ref, *refs
):
    outs, (mid, blocks, edges, inv, cnt, where, sems) = refs[:-7], refs[-7:]
    rows, columns = x_ref.shape
    slabs, tiles = columns // LANES, rows // SUB
    own = own_ref[0]
    lane = lane_ids()

    for e in range(devices * cap):
        inv[e] = 0
    for p in range(devices):
        cnt[p] = 0

    def book(b):
        p = tgt_ref[own, b]
        c = cnt[p]
        cnt[p] = c + 1
        k = jnp.bitwise_xor(p, own) if paired else p
        at = k * cap + jnp.minimum(c, cap - 1)
        inv[at] = b
        where[b] = at

    col_w = tap_weights(shift_ref[visit, 0, 1], frac_ref[visit, 0, 1], lane)
    row_w = tap_weights(shift_ref[visit, 0, 0], frac_ref[visit, 0, 0], lane)
    for j in range(slabs):
        mid[j, 0:SUB, :] = jnp.zeros((SUB, LANES), jnp.float32)
        mid[j, SUB + rows :, :] = jnp.zeros((SUB, LANES), jnp.float32)

    def column_pass(t):
        for b in range(NB // tiles):
            book(t * (NB // tiles) + b)
        at = pl.multiple_of(t * SUB, SUB)
        parts = [x_ref[pl.ds(at, SUB), j * LANES : (j + 1) * LANES] for j in range(slabs)]
        zero = jnp.zeros((SUB, LANES), jnp.float32)
        ahead = [shifted([zero] + parts, -b, lane) for b in range(STEP)]
        total = [zero] * slabs
        for a in sorted({d // STEP for d in TAPS}):
            group = [zero] * (slabs + 1)
            for n, d in enumerate(TAPS):
                if d // STEP == a:
                    group = [g + col_w[n] * m for g, m in zip(group, ahead[d - STEP * a])]
            moved = shifted(group, -STEP * a, lane)[1:]
            total = [x + m for x, m in zip(total, moved)]
        for j in range(slabs):
            mid[j, pl.ds(at + SUB, SUB), :] = total[j]

    @pl.loop(0, rows // BR)
    def _(band):
        for t in range(BR // SUB):
            column_pass(band * (BR // SUB) + t)

    def send(b):
        p, r = lax.div(where[b], cap), lax.rem(where[b], cap)
        to = outs[0].at[p, pl.ds(pl.multiple_of(r * BR, BR), BR), :]
        return pltpu.make_async_copy(blocks.at[b], to, sems.at[b])

    @pl.loop(0, slabs)
    def _(j):
        for t in range(tiles):
            first = SUB + t * SUB
            total = jnp.zeros((SUB, LANES), jnp.float32)
            for n, d in enumerate(TAPS):
                total = total + row_w[n] * mid[j, first + d : first + d + SUB, :]
            inner = (t * SUB) % BR
            blocks[(t * SUB) // BR * slabs + j, inner : inner + SUB, :] = total
        if not paired:
            for band in range(rows // BR):
                send(band * slabs + j).start()

    if paired:
        for k in range(devices):
            for r in range(cap):
                outs[k][r * BR : (r + 1) * BR, :] = blocks[inv[k * cap + r]]
        return

    @pl.loop(0, devices)
    def _(p):
        before, after = jnp.maximum(p - 1, 0), jnp.minimum(p + 1, devices - 1)
        edges[p] = jnp.zeros((2 * SUB, LANES), jnp.float32)
        for r in range(cap):
            at = REACH * r
            edges[p, at : at + REACH, :] = blocks[inv[before * cap + r], BR - REACH : BR, :]
            at = SUB + REACH * r
            edges[p, at : at + REACH, :] = blocks[inv[after * cap + r], 0:REACH, :]

    last = pltpu.make_async_copy(edges, outs[0].at[:, cap * BR :, :], sems.at[NB])
    last.start()
    last.wait()

    @pl.loop(0, NB)
    def _(b):
        send(b).wait()


def sum_blocks(devices, cap, paired, own, table_ref, ins, acc):
    acc[...] = jnp.zeros_like(acc)

    def add(chunk, c):
        for r in range(cap):
            slot = table_ref[c * cap + r]
            acc[slot] = acc[slot] + chunk[r * BR : (r + 1) * BR, :]

    if paired:
        for k in range(devices):
            add(ins[k], jnp.bitwise_xor(own, k))
    else:

        @pl.loop(0, devices)
        def _(c):
            add(ins[0].at[c], c)


def template_kernel(
    devices, cap, paired, own_ref, table_ref, ends_ref, edges_ref, coef_ref, *refs
):
    ins, (cols_ref, gram_ref, acc, far, gen, spec) = refs[:-6], refs[-6:]
    slabs, rows = cols_ref.shape[1], cols_ref.shape[2] - 2 * SUB
    ext_ref = cols_ref.at[REACH]

    def lagged(lag):
        if abs(lag) <= REACH:
            return cols_ref.at[REACH - lag]
        return far.at[lag + KSIDE - 1 if lag < 0 else lag + KSIDE - 1 - KSIDE]

    tiles = rows // SUB
    lane = lane_ids()
    sub = lax.broadcasted_iota(jnp.int32, (SUB, LANES), 0)
    sum_blocks(devices, cap, paired, own_ref[0], table_ref, ins, acc)

    for end in range(2):
        at = cap * BR + end * SUB
        if paired:
            strip = jnp.concatenate([chunk[at : at + SUB, :] for chunk in ins], axis=0)
        else:
            strip = ins[0][:, at : at + SUB, :].reshape(devices * SUB, LANES)
        edge = mm(edges_ref[end], strip)
        first = SUB - REACH if end == 0 else SUB + rows
        for j in range(slabs):
            whole = 0 if end == 0 else SUB + rows
            ext_ref[j, whole : whole + SUB, :] = jnp.zeros((SUB, LANES), jnp.float32)
            for i in range(REACH):
                ext_ref[j, first + i : first + i + 1, :] = edge[i * slabs + j : i * slabs + j + 1]

    def lag_tile(parts, at):
        for lag in LAGS:
            for j, moved in enumerate(shifted(parts, lag, lane)):
                lagged(lag)[j, at, :] = moved

    for at in (slice(0, SUB), slice(SUB + rows, 2 * SUB + rows)):
        lag_tile([ext_ref[j, at, :] for j in range(slabs)], at)
    for band in range(rows // BR):

        @pl.loop(0, BR // SUB, unroll=UNROLL)
        def _(t):
            at = pl.ds(pl.multiple_of(t * SUB, SUB), SUB)
            to = pl.ds(pl.multiple_of(SUB + band * BR + t * SUB, SUB), SUB)
            parts = [acc[band * slabs + j, at, :] for j in range(slabs)]
            lag_tile(parts, to)

    gen[...] = jnp.zeros_like(gen)
    spec[...] = jnp.zeros_like(spec)

    @pl.loop(0, slabs)
    def _(j):
        def first(t, down, lag):
            base = SUB + t * SUB - down // 2
            return lagged(lag)[j, base : base + SUB, :]

        def second(t, down):
            base = SUB + t * SUB + down
            return ext_ref[j, base : base + SUB, :]

        sums = [None] * len(PRODUCTS)
        for t in range(tiles):
            moved = [second(t, down - down // 2) for down in range(KSIDE)]
            for n, (down, lag) in enumerate(PRODUCTS):
                term = first(t, down, lag) * moved[down]
                sums[n] = term if sums[n] is None else sums[n] + term
        edge = ((j == 0) & (lane < REACH)) | ((j == slabs - 1) & (lane >= LANES - REACH))
        for n in range(len(PRODUCTS)):
            gen[n] = gen[n] + jnp.where(edge, 0.0, sums[n])
            spec[n] = spec[n] + jnp.where(edge, sums[n], 0.0)
        for m, (row, down, lag) in enumerate(EDGES):
            n = len(PRODUCTS) + m
            t = 0 if row >= 0 else tiles - 1
            here = (sub == row % SUB) & (ends_ref[0 if row >= 0 else 1] > 0)
            term = first(t, 0, lag) * second(t, down)
            term = jnp.where(here, term, 0.0)
            gen[n] = gen[n] + jnp.where(edge, 0.0, term)
            spec[n] = spec[n] + jnp.where(edge, term, 0.0)

    src = lax.broadcasted_iota(jnp.int32, (LANES, LANES), 0)
    q2 = lax.rem(lax.broadcasted_iota(jnp.int32, (LANES, LANES), 1), KSIDE)
    late = (src >= REACH) & (q2 - REACH >= src - (LANES - 1))
    inside = jnp.where(((src < REACH) & (q2 - REACH <= src)) | late, 1.0, 0.0)
    data = mm(jnp.sum(gen[...], axis=1), jnp.ones((LANES, LANES), jnp.float32))
    data = data + mm(jnp.sum(spec[...], axis=1), inside)
    gram_ref[...] = jnp.zeros_like(gram_ref)
    for i in range(KB):
        gram_ref[i : i + 1, :] = jnp.sum(coef_ref[i] * data, axis=0, keepdims=True)
    total = gram_ref[...]
    size = total.shape[0]
    below = jnp.zeros((LANES - size, LANES), jnp.float32)
    flipped = jnp.transpose(jnp.concatenate([total, below], axis=0))[:size]
    row = lax.broadcasted_iota(jnp.int32, (size, LANES), 0)
    column = lax.broadcasted_iota(jnp.int32, (size, LANES), 1)
    gram_ref[...] = total + jnp.where(row == column, 0.0, flipped)


def science_kernel(devices, cap, paired, own_ref, table_ref, cols_ref, gram_ref, *refs):
    ins, (out, fit_ref, sums_ref) = refs[:-3], refs[-3:]
    slabs, rows = cols_ref.shape[1], cols_ref.shape[2] - 2 * SUB
    sum_blocks(devices, cap, paired, own_ref[0], table_ref, ins, out)

    sums_ref[...] = jnp.zeros_like(sums_ref)

    @pl.loop(0, slabs)
    def _(j):
        sums = [None] * KB
        for t in range(rows // SUB):
            base = SUB + t * SUB - REACH
            inner = (t * SUB) % BR
            target = out[(t * SUB) // BR * slabs + j, inner : inner + SUB, :]
            for r in range(KSIDE):
                for q in range(KSIDE):
                    i = r * KSIDE + q
                    term = cols_ref[q, j, base + r : base + r + SUB, :] * target
                    sums[i] = term if sums[i] is None else sums[i] + term
        for i in range(KB):
            sums_ref[i] = sums_ref[i] + sums[i]

    rhs = jnp.sum(jnp.sum(sums_ref[...], axis=1), axis=1, keepdims=True)
    size = gram_ref.shape[0]
    column = lax.broadcasted_iota(jnp.int32, (size, LANES), 1)
    joined = jnp.where(column == RHS_LANE, rhs, gram_ref[...])
    packed = joined[0:SUB]
    for a in range(1, size // SUB):
        packed = packed + pltpu.roll(joined[a * SUB : (a + 1) * SUB], a * size, 1)
    for k in range(devices):
        fit_ref[k] = packed


def solved(packed, size):
    parts = [packed] + [
        pltpu.roll(packed, LANES - a * size, 1) for a in range(1, size // SUB)
    ]
    work = jnp.concatenate(parts, axis=0)
    row = lax.broadcasted_iota(jnp.int32, (size, LANES), 0)
    lane = lax.broadcasted_iota(jnp.int32, (size, LANES), 1)
    diagonal = (row == lane) & (row < KB)
    trace = jnp.sum(jnp.where(diagonal, work, 0.0), axis=(0, 1), keepdims=True)
    ridge = 0.001 * trace / KB + 1.0
    work = jnp.where(lane < size, jnp.where(diagonal, work + ridge, work), 0.0)
    for base in range(0, KB, GROUP):
        group = [
            jnp.broadcast_to(work[:, i : i + 1], (size, LANES)) for i in range(base, base + GROUP)
        ]
        for k, column in enumerate(group):
            i = base + k
            inverse = 1.0 / column[i : i + 1]

            def eliminated(values):
                pivot = values[i : i + 1] * inverse
                return jnp.where(row == i, pivot, values - column * pivot)

            group[k + 1 :] = [eliminated(c) for c in group[k + 1 :]]
            work = eliminated(work)
    return work[:, RHS_LANE : RHS_LANE + 1]


def difference_kernel(fit_ref, cols_ref, sci_ref, out_ref):
    slabs, rows = cols_ref.shape[1], cols_ref.shape[2] - 2 * SUB
    shared = fit_ref[0]
    for k in range(1, fit_ref.shape[0]):
        shared = shared + fit_ref[k]
    kernel = solved(shared, NB)
    taps = [jnp.broadcast_to(kernel[i : i + 1, :], (SUB, LANES)) for i in range(KB)]

    @pl.loop(0, rows // BR)
    def _(band):
        for j in range(slabs):
            for t in range(BR // SUB):
                total = None
                for r in range(KSIDE):
                    for q in range(KSIDE):
                        at = pl.ds(band * BR + SUB + t * SUB + r - REACH, SUB)
                        term = taps[r * KSIDE + q] * cols_ref[q, j, at, :]
                        total = term if total is None else total + term
                science = sci_ref[band * slabs + j, t * SUB : (t + 1) * SUB, :]
                at = pl.ds(pl.multiple_of(band * BR + t * SUB, SUB), SUB)
                out_ref[at, j * LANES : (j + 1) * LANES] = science - total


def by_permutes(devices):
    return devices <= MAX_PERMUTES and devices & (devices - 1) == 0


def gram_table():
    count = -(-(len(PRODUCTS) + len(EDGES)) // SUB) * SUB
    coef = np.zeros((KB, count, LANES), np.float32)
    left_out = {0: (-2, -1), 1: (-1,), 2: (), 3: (0,), 4: (0, 1)}
    for r in range(KSIDE):
        for q in range(KSIDE):
            for n, (row, down, lag) in enumerate([(None, *p) for p in PRODUCTS] + list(EDGES)):
                if r + down < KSIDE and 0 <= q + lag < KSIDE:
                    column = (r + down) * KSIDE + q + lag
                    if row is None:
                        coef[r * KSIDE + q, n, column] = 1.0
                    elif row in left_out[r]:
                        coef[r * KSIDE + q, n, column] = -1.0
    return count, coef


def body(exposures, lanczos_shift, lanczos_frac, margin_patch, margin_slot):
    rows, columns = exposures.shape[1], exposures.shape[2]
    slabs = columns // LANES
    devices = lax.axis_size("ccd")
    owner = lax.axis_index("ccd")
    cap = max(2, 2 * NB // devices)
    paired = by_permutes(devices)
    own = owner.astype(jnp.int32).reshape(1)
    targets = margin_patch[:, :, 0]

    pixels = rows * columns

    def warped(visit, paired):
        packed = [f32(cap * BR, BC)] * devices if paired else [f32(devices, cap * BR + 2 * SUB, BC)]
        return call(
            functools.partial(warp_kernel, visit, devices, cap, paired),
            packed,
            [SMEM, SMEM, SMEM, SMEM, pl.BlockSpec((None, rows, columns), lambda i: (visit, 0, 0))],
            [
                pltpu.VMEM((slabs, rows + 2 * SUB, LANES), jnp.float32),
                pltpu.VMEM((NB, BR, BC), jnp.float32),
                pltpu.VMEM((devices, 2 * SUB, LANES), jnp.float32),
                pltpu.SMEM((devices * cap,), jnp.int32),
                pltpu.SMEM((devices,), jnp.int32),
                pltpu.SMEM((NB,), jnp.int32),
                pltpu.SemaphoreType.DMA((NB + 1,)),
            ],
            40 * pixels,
            4 * pixels * 3,
            grid=(1,),
            room=0 if visit == 0 else 16,
            out=VMEM if paired else pl.BlockSpec(memory_space=pltpu.HBM),
        )(own, targets, lanczos_shift, lanczos_frac, exposures)

    def exchanged(chunks):
        if len(chunks) == 1:
            return [lax.all_to_all(chunks[0], "ccd", split_axis=0, concat_axis=0, tiled=True)]
        moved = [chunks[0]]
        for k in range(1, devices):
            moved.append(
                lax.ppermute(chunks[k], "ccd", [(i, i ^ k) for i in range(devices)])
            )
        return moved

    template_chunks = warped(0, False)
    science_chunks = warped(1, paired)
    template_in = exchanged(template_chunks)
    science_in = exchanged(science_chunks)

    block_ids = jnp.arange(NB)
    earlier = block_ids[None, :] < block_ids[:, None]
    same = targets[:, :, None] == targets[:, None, :]
    order = jnp.sum(same & earlier[None], axis=2)
    in_place = order[:, None, :] == jnp.arange(cap)[None, :, None]

    def slots_at(patch):
        arrives = (targets == patch)[:, None, :] & in_place
        slots = jnp.sum(jnp.where(arrives, margin_slot[:, None, :], 0), axis=2)
        return jnp.where(jnp.any(arrives, axis=2), slots, NB).astype(jnp.int32)

    table = slots_at(owner).reshape(-1)
    wanted = jnp.arange(REACH * slabs)[:, None, None, None]
    row_of = jnp.arange(SUB // REACH * REACH).reshape(1, 1, SUB // REACH, REACH) % REACH
    spare = ((0, 0), (0, SUB // REACH - cap))

    def edge_rows(patch, first_slot):
        slots = jnp.pad(slots_at(patch), spare, constant_values=NB)
        slots = slots[None, :, :, None]
        hit = (slots - first_slot == wanted % slabs) & (row_of == wanted // slabs)
        return hit.astype(jnp.float32).reshape(REACH * slabs, devices * SUB)

    edges = jnp.stack([edge_rows(owner - 1, NB - slabs), edge_rows(owner + 1, 0)])

    sums = pltpu.VMEM((NB + 1, BR, BC), jnp.float32)
    size = NB
    count, coef = gram_table()
    at_ends = jnp.stack([owner == 0, owner == devices - 1]).astype(jnp.int32)
    shifts, gram = call(
        functools.partial(template_kernel, devices, cap, False),
        [f32(KSIDE, slabs, rows + 2 * SUB, LANES), f32(size, LANES)],
        [SMEM, SMEM, SMEM] + [VMEM] * (2 + len(template_in)),
        [
            sums,
            pltpu.VMEM((len(LAGS) - KSIDE, slabs, rows + 2 * SUB, LANES), jnp.float32),
            pltpu.VMEM((count, SUB, LANES), jnp.float32),
            pltpu.VMEM((count, SUB, LANES), jnp.float32),
        ],
        pixels * 2 * len(PRODUCTS),
        pixels * 8,
    )(own, table, at_ends, edges, jnp.asarray(coef), *template_in)

    science, fit = call(
        functools.partial(science_kernel, devices, cap, paired),
        [f32(NB + 1, BR, BC), f32(devices, SUB, LANES)],
        [SMEM, SMEM, VMEM, VMEM] + [VMEM] * len(science_in),
        [pltpu.VMEM((size, SUB, LANES), jnp.float32)],
        pixels * 2 * KB,
        pixels * 16,
    )(own, table, shifts, gram, *science_in)
    fit = lax.all_to_all(fit, "ccd", split_axis=0, concat_axis=0, tiled=True)

    return call(
        difference_kernel, f32(rows, columns), [VMEM] * 3, [], pixels * 2 * KB, pixels * 12
    )(fit, shifts, science)


def solution(mesh):
    placed = (
        P(None, ("field", "ccd"), None),
        P(None, ("field", "ccd"), None),
        P(None, ("field", "ccd"), None),
        P("field", None, None),
        P("field", None),
    )
    return jax.shard_map(
        body, mesh=mesh, in_specs=placed, out_specs=P(("field", "ccd"), None), check_vma=False
    )
```

```python
import functools

import jax
import jax.numpy as jnp
import numpy as np
from jax import lax
from jax.experimental import pallas as pl
from jax.experimental.pallas import tpu as pltpu
from jax.sharding import PartitionSpec as P


BR = 32
BC = 128
KSIDE = 5
KB = 25
NB = 32
REACH = KSIDE // 2
SUB = 8
LANES = 128
TAP_LOW, TAP_HIGH = -4, 5
TAPS = tuple(range(TAP_LOW, TAP_HIGH + 1))
LAGS = tuple(range(-(KSIDE - 1), KSIDE))
PRODUCTS = tuple(
    (down, lag) for down in range(KSIDE) for lag in (range(KSIDE) if down == 0 else LAGS)
)
EDGE_ROWS = ((0, (0, 1)), (1, (0,)), (-2, (0, 1)), (-1, (0,)))
EDGES = tuple(
    (row, down, lag) for row, downs in EDGE_ROWS for down, lag in PRODUCTS if down in downs
)
MAX_PERMUTES = 32
UNROLL = 4
STEP = 4
GROUP = 5
LATE = 2
RHS_LANE = KB


HIGHEST = lax.Precision.HIGHEST
SMEM = pl.BlockSpec(memory_space=pltpu.SMEM)
VMEM = pl.BlockSpec(memory_space=pltpu.VMEM)


def mm(a, b, contract=((1,), (0,))):
    return lax.dot_general(
        a, b, (contract, ((), ())), precision=HIGHEST, preferred_element_type=jnp.float32
    )


def call(kernel, out_shape, in_specs, scratch, flops, moved, grid=(), room=16, out=VMEM):
    many = isinstance(out_shape, (list, tuple))
    return pl.pallas_call(
        kernel,
        out_shape=out_shape,
        grid=grid,
        in_specs=in_specs,
        out_specs=[out] * len(out_shape) if many else out,
        scratch_shapes=scratch,
        cost_estimate=pl.CostEstimate(flops=flops, bytes_accessed=moved, transcendentals=0),
        compiler_params=pltpu.CompilerParams(vmem_limit_bytes=room << 20 if room else None),
    )


def f32(*shape):
    return jax.ShapeDtypeStruct(shape, jnp.float32)


def lane_ids():
    return lax.broadcasted_iota(jnp.int32, (SUB, LANES), 1)


def shifted(parts, by, lane):
    if by == 0:
        return list(parts)
    turned = [pltpu.roll(part, by % LANES, 1) for part in parts]
    zero = jnp.zeros_like(parts[0])
    out = []
    for j in range(len(parts)):
        beside = j - 1 if by > 0 else j + 1
        other = turned[beside] if 0 <= beside < len(parts) else zero
        keep = lane >= by if by > 0 else lane < LANES + by
        out.append(jnp.where(keep, turned[j], other))
    return out


def sinc(t):
    scaled = jnp.float32(np.pi) * t
    safe = jnp.where(t == 0.0, jnp.float32(1.0), scaled)
    return jnp.where(t == 0.0, jnp.float32(1.0), jnp.sin(safe) / safe)


def tap_weights(shift, frac, lane):
    t = (lane + TAP_LOW).astype(jnp.float32) - shift.astype(jnp.float32) - frac
    w = jnp.where(jnp.abs(t) < 3.0, sinc(t) * sinc(t / 3.0), 0.0)
    return [jnp.broadcast_to(w[:, k : k + 1], (SUB, LANES)) for k in range(len(TAPS))]


def warp_kernel(
    visit, devices, cap, paired, own_ref, tgt_ref, shift_ref, frac_ref, x_ref, *refs
):
    outs, (mid, blocks, edges, inv, cnt, where, sems) = refs[:-7], refs[-7:]
    rows, columns = x_ref.shape
    slabs, tiles = columns // LANES, rows // SUB
    own = own_ref[0]
    lane = lane_ids()

    for e in range(devices * cap):
        inv[e] = 0
    for p in range(devices):
        cnt[p] = 0

    def book(b):
        p = tgt_ref[own, b]
        c = cnt[p]
        cnt[p] = c + 1
        k = jnp.bitwise_xor(p, own) if paired else p
        at = k * cap + jnp.minimum(c, cap - 1)
        inv[at] = b
        where[b] = at

    col_w = tap_weights(shift_ref[visit, 0, 1], frac_ref[visit, 0, 1], lane)
    row_w = tap_weights(shift_ref[visit, 0, 0], frac_ref[visit, 0, 0], lane)
    for j in range(slabs):
        mid[j, 0:SUB, :] = jnp.zeros((SUB, LANES), jnp.float32)
        mid[j, SUB + rows :, :] = jnp.zeros((SUB, LANES), jnp.float32)

    def column_pass(t):
        for b in range(NB // tiles):
            book(t * (NB // tiles) + b)
        at = pl.multiple_of(t * SUB, SUB)
        parts = [x_ref[pl.ds(at, SUB), j * LANES : (j + 1) * LANES] for j in range(slabs)]
        zero = jnp.zeros((SUB, LANES), jnp.float32)
        ahead = [shifted([zero] + parts, -b, lane) for b in range(STEP)]
        total = [zero] * slabs
        for a in sorted({d // STEP for d in TAPS}):
            group = [zero] * (slabs + 1)
            for n, d in enumerate(TAPS):
                if d // STEP == a:
                    group = [g + col_w[n] * m for g, m in zip(group, ahead[d - STEP * a])]
            moved = shifted(group, -STEP * a, lane)[1:]
            total = [x + m for x, m in zip(total, moved)]
        for j in range(slabs):
            mid[j, pl.ds(at + SUB, SUB), :] = total[j]

    @pl.loop(0, rows // BR)
    def _(band):
        for t in range(BR // SUB):
            column_pass(band * (BR // SUB) + t)

    def send(b):
        p, r = lax.div(where[b], cap), lax.rem(where[b], cap)
        to = outs[0].at[p, pl.ds(pl.multiple_of(r * BR, BR), BR), :]
        return pltpu.make_async_copy(blocks.at[b], to, sems.at[b])

    @pl.loop(0, slabs)
    def _(j):
        for t in range(tiles):
            first = SUB + t * SUB
            total = jnp.zeros((SUB, LANES), jnp.float32)
            for n, d in enumerate(TAPS):
                total = total + row_w[n] * mid[j, first + d : first + d + SUB, :]
            inner = (t * SUB) % BR
            blocks[(t * SUB) // BR * slabs + j, inner : inner + SUB, :] = total
        if not paired:
            for band in range(rows // BR):
                send(band * slabs + j).start()

    if paired:
        for k in range(devices):
            for r in range(cap):
                outs[k][r * BR : (r + 1) * BR, :] = blocks[inv[k * cap + r]]
        return

    @pl.loop(0, devices)
    def _(p):
        before, after = jnp.maximum(p - 1, 0), jnp.minimum(p + 1, devices - 1)
        edges[p] = jnp.zeros((2 * SUB, LANES), jnp.float32)
        for r in range(cap):
            at = REACH * r
            edges[p, at : at + REACH, :] = blocks[inv[before * cap + r], BR - REACH : BR, :]
            at = SUB + REACH * r
            edges[p, at : at + REACH, :] = blocks[inv[after * cap + r], 0:REACH, :]

    last = pltpu.make_async_copy(edges, outs[0].at[:, cap * BR :, :], sems.at[NB])
    last.start()
    last.wait()

    @pl.loop(0, NB)
    def _(b):
        send(b).wait()


def sum_blocks(devices, cap, paired, own, table_ref, ins, acc):
    acc[...] = jnp.zeros_like(acc)

    def add(chunk, c):
        for r in range(cap):
            slot = table_ref[c * cap + r]
            acc[slot] = acc[slot] + chunk[r * BR : (r + 1) * BR, :]

    if paired:
        for k, chunk in enumerate(ins):
            add(chunk, jnp.bitwise_xor(own, k))
    else:

        @pl.loop(0, devices)
        def _(c):
            add(ins[0].at[c], c)


def template_kernel(
    devices, cap, paired, own_ref, table_ref, ends_ref, edges_ref, coef_ref, *refs
):
    ins, (cols_ref, gram_ref, acc, far, gen, spec) = refs[:-6], refs[-6:]
    slabs, rows = cols_ref.shape[1], cols_ref.shape[2] - 2 * SUB
    ext_ref = cols_ref.at[REACH]

    def lagged(lag):
        if abs(lag) <= REACH:
            return cols_ref.at[REACH - lag]
        return far.at[lag + KSIDE - 1 if lag < 0 else lag + KSIDE - 1 - KSIDE]

    tiles = rows // SUB
    lane = lane_ids()
    sub = lax.broadcasted_iota(jnp.int32, (SUB, LANES), 0)
    sum_blocks(devices, cap, paired, own_ref[0], table_ref, ins, acc)

    for end in range(2):
        at = cap * BR + end * SUB
        if paired:
            strip = jnp.concatenate([chunk[at : at + SUB, :] for chunk in ins], axis=0)
        else:
            strip = ins[0][:, at : at + SUB, :].reshape(devices * SUB, LANES)
        edge = mm(edges_ref[end], strip)
        first = SUB - REACH if end == 0 else SUB + rows
        for j in range(slabs):
            whole = 0 if end == 0 else SUB + rows
            ext_ref[j, whole : whole + SUB, :] = jnp.zeros((SUB, LANES), jnp.float32)
            for i in range(REACH):
                ext_ref[j, first + i : first + i + 1, :] = edge[i * slabs + j : i * slabs + j + 1]

    def lag_tile(parts, at):
        for lag in LAGS:
            for j, moved in enumerate(shifted(parts, lag, lane)):
                lagged(lag)[j, at, :] = moved

    for at in (slice(0, SUB), slice(SUB + rows, 2 * SUB + rows)):
        lag_tile([ext_ref[j, at, :] for j in range(slabs)], at)
    for band in range(rows // BR):

        @pl.loop(0, BR // SUB, unroll=UNROLL)
        def _(t):
            at = pl.ds(pl.multiple_of(t * SUB, SUB), SUB)
            to = pl.ds(pl.multiple_of(SUB + band * BR + t * SUB, SUB), SUB)
            parts = [acc[band * slabs + j, at, :] for j in range(slabs)]
            lag_tile(parts, to)

    gen[...] = jnp.zeros_like(gen)
    spec[...] = jnp.zeros_like(spec)

    @pl.loop(0, slabs)
    def _(j):
        def first(t, down, lag):
            base = SUB + t * SUB - down // 2
            return lagged(lag)[j, base : base + SUB, :]

        def second(t, down):
            base = SUB + t * SUB + down
            return ext_ref[j, base : base + SUB, :]

        sums = [None] * len(PRODUCTS)
        for t in range(tiles):
            moved = [second(t, down - down // 2) for down in range(KSIDE)]
            for n, (down, lag) in enumerate(PRODUCTS):
                term = first(t, down, lag) * moved[down]
                sums[n] = term if sums[n] is None else sums[n] + term
        edge = ((j == 0) & (lane < REACH)) | ((j == slabs - 1) & (lane >= LANES - REACH))
        for n in range(len(PRODUCTS)):
            gen[n] = gen[n] + jnp.where(edge, 0.0, sums[n])
            spec[n] = spec[n] + jnp.where(edge, sums[n], 0.0)
        for m, (row, down, lag) in enumerate(EDGES):
            n = len(PRODUCTS) + m
            t = 0 if row >= 0 else tiles - 1
            here = (sub == row % SUB) & (ends_ref[0 if row >= 0 else 1] > 0)
            term = first(t, 0, lag) * second(t, down)
            term = jnp.where(here, term, 0.0)
            gen[n] = gen[n] + jnp.where(edge, 0.0, term)
            spec[n] = spec[n] + jnp.where(edge, term, 0.0)

    src = lax.broadcasted_iota(jnp.int32, (LANES, LANES), 0)
    q2 = lax.rem(lax.broadcasted_iota(jnp.int32, (LANES, LANES), 1), KSIDE)
    late = (src >= REACH) & (q2 - REACH >= src - (LANES - 1))
    inside = jnp.where(((src < REACH) & (q2 - REACH <= src)) | late, 1.0, 0.0)
    data = mm(jnp.sum(gen[...], axis=1), jnp.ones((LANES, LANES), jnp.float32))
    data = data + mm(jnp.sum(spec[...], axis=1), inside)
    gram_ref[...] = jnp.zeros_like(gram_ref)
    for i in range(KB):
        gram_ref[i : i + 1, :] = jnp.sum(coef_ref[i] * data, axis=0, keepdims=True)
    total = gram_ref[...]
    size = total.shape[0]
    below = jnp.zeros((LANES - size, LANES), jnp.float32)
    flipped = jnp.transpose(jnp.concatenate([total, below], axis=0))[:size]
    row = lax.broadcasted_iota(jnp.int32, (size, LANES), 0)
    column = lax.broadcasted_iota(jnp.int32, (size, LANES), 1)
    gram_ref[...] = total + jnp.where(row == column, 0.0, flipped)


def joined_fit(gram, sums):
    rhs = jnp.sum(jnp.sum(sums, axis=1), axis=1, keepdims=True)
    size = gram.shape[0]
    column = lax.broadcasted_iota(jnp.int32, (size, LANES), 1)
    joined = jnp.where(column == RHS_LANE, rhs, gram)
    packed = joined[0:SUB]
    for a in range(1, size // SUB):
        packed = packed + pltpu.roll(joined[a * SUB : (a + 1) * SUB], a * size, 1)
    return packed


def science_kernel(devices, cap, paired, own_ref, table_ref, cols_ref, *refs):
    ins, (out, sums_ref) = refs[:-2], refs[-2:]
    slabs, rows = cols_ref.shape[1], cols_ref.shape[2] - 2 * SUB
    sum_blocks(devices, cap, paired, own_ref[0], table_ref, ins, out)
    sums_ref[...] = jnp.zeros_like(sums_ref)

    @pl.loop(0, slabs)
    def _(j):
        sums = [None] * KB
        for t in range(rows // SUB):
            base = SUB + t * SUB - REACH
            inner = (t * SUB) % BR
            target = out[(t * SUB) // BR * slabs + j, inner : inner + SUB, :]
            for r in range(KSIDE):
                for q in range(KSIDE):
                    i = r * KSIDE + q
                    term = cols_ref[q, j, base + r : base + r + SUB, :] * target
                    sums[i] = term if sums[i] is None else sums[i] + term
        for i in range(KB):
            sums_ref[i] = sums_ref[i] + sums[i]


def late_kernel(
    first, cap, own_ref, table_ref, cols_ref, gram_ref, early_ref, sums_ref, *refs
):
    ins, (out, fit_ref, all_sums) = refs[:-3], refs[-3:]
    slabs = cols_ref.shape[1]
    out[...] = early_ref[...]
    sums = [sums_ref[i] for i in range(KB)]
    for n, chunk in enumerate(ins):
        for r in range(cap):
            slot = table_ref[jnp.bitwise_xor(own_ref[0], first + n) * cap + r]
            out[slot] = out[slot] + chunk[r * BR : (r + 1) * BR, :]
            share = (slot < NB).astype(jnp.float32)
            inside = jnp.minimum(slot, NB - 1)
            j, band = lax.rem(inside, slabs), lax.div(inside, slabs)
            for t in range(BR // SUB):
                at = r * BR + t * SUB
                target = chunk[at : at + SUB, :] * share
                base = band * BR + SUB + t * SUB - REACH
                for i in range(KB):
                    part = cols_ref[i % KSIDE, j, pl.ds(base + i // KSIDE, SUB), :]
                    sums[i] = sums[i] + part * target
    all_sums[...] = jnp.zeros_like(all_sums)
    for i in range(KB):
        all_sums[i] = sums[i]
    packed = joined_fit(gram_ref[...], all_sums[...])
    for k in range(fit_ref.shape[0]):
        fit_ref[k] = packed


def fit_kernel(gram_ref, sums_ref, fit_ref):
    packed = joined_fit(gram_ref[...], sums_ref[...])
    for k in range(fit_ref.shape[0]):
        fit_ref[k] = packed


def solved(packed, size):
    parts = [packed] + [
        pltpu.roll(packed, LANES - a * size, 1) for a in range(1, size // SUB)
    ]
    work = jnp.concatenate(parts, axis=0)
    row = lax.broadcasted_iota(jnp.int32, (size, LANES), 0)
    lane = lax.broadcasted_iota(jnp.int32, (size, LANES), 1)
    diagonal = (row == lane) & (row < KB)
    trace = jnp.sum(jnp.where(diagonal, work, 0.0), axis=(0, 1), keepdims=True)
    ridge = 0.001 * trace / KB + 1.0
    work = jnp.where(lane < size, jnp.where(diagonal, work + ridge, work), 0.0)
    for base in range(0, KB, GROUP):
        group = [
            jnp.broadcast_to(work[:, i : i + 1], (size, LANES)) for i in range(base, base + GROUP)
        ]
        for k, column in enumerate(group):
            i = base + k
            inverse = 1.0 / column[i : i + 1]

            def eliminated(values):
                pivot = values[i : i + 1] * inverse
                return jnp.where(row == i, pivot, values - column * pivot)

            group[k + 1 :] = [eliminated(c) for c in group[k + 1 :]]
            work = eliminated(work)
    return work[:, RHS_LANE : RHS_LANE + 1]


def difference_kernel(fit_ref, cols_ref, sci_ref, out_ref, whole, sems):
    slabs, rows = cols_ref.shape[1], cols_ref.shape[2] - 2 * SUB
    shared = fit_ref[0]
    for k in range(1, fit_ref.shape[0]):
        shared = shared + fit_ref[k]
    kernel = solved(shared, NB)
    taps = [jnp.broadcast_to(kernel[i : i + 1, :], (SUB, LANES)) for i in range(KB)]

    def store(band):
        at = pl.ds(pl.multiple_of(band * BR, BR), BR)
        return pltpu.make_async_copy(whole.at[at, :], out_ref.at[at, :], sems.at[band])

    @pl.loop(0, rows // BR)
    def _(band):
        for j in range(slabs):
            for t in range(BR // SUB):
                total = None
                for r in range(KSIDE):
                    for q in range(KSIDE):
                        at = pl.ds(band * BR + SUB + t * SUB + r - REACH, SUB)
                        term = taps[r * KSIDE + q] * cols_ref[q, j, at, :]
                        total = term if total is None else total + term
                science = sci_ref[band * slabs + j, t * SUB : (t + 1) * SUB, :]
                at = pl.ds(pl.multiple_of(band * BR + t * SUB, SUB), SUB)
                whole[at, j * LANES : (j + 1) * LANES] = science - total
        store(band).start()

    for band in range(rows // BR):
        store(band).wait()


def by_permutes(devices):
    return devices <= MAX_PERMUTES and devices & (devices - 1) == 0


def gram_table():
    count = -(-(len(PRODUCTS) + len(EDGES)) // SUB) * SUB
    coef = np.zeros((KB, count, LANES), np.float32)
    left_out = {0: (-2, -1), 1: (-1,), 2: (), 3: (0,), 4: (0, 1)}
    for r in range(KSIDE):
        for q in range(KSIDE):
            for n, (row, down, lag) in enumerate([(None, *p) for p in PRODUCTS] + list(EDGES)):
                if r + down < KSIDE and 0 <= q + lag < KSIDE:
                    column = (r + down) * KSIDE + q + lag
                    if row is None:
                        coef[r * KSIDE + q, n, column] = 1.0
                    elif row in left_out[r]:
                        coef[r * KSIDE + q, n, column] = -1.0
    return count, coef


def body(exposures, lanczos_shift, lanczos_frac, margin_patch, margin_slot):
    rows, columns = exposures.shape[1], exposures.shape[2]
    slabs = columns // LANES
    devices = lax.axis_size("ccd")
    owner = lax.axis_index("ccd")
    cap = max(2, 2 * NB // devices)
    paired = by_permutes(devices)
    own = owner.astype(jnp.int32).reshape(1)
    targets = margin_patch[:, :, 0]

    pixels = rows * columns

    def warped(visit, paired):
        packed = [f32(cap * BR, BC)] * devices if paired else [f32(devices, cap * BR + 2 * SUB, BC)]
        return call(
            functools.partial(warp_kernel, visit, devices, cap, paired),
            packed,
            [SMEM, SMEM, SMEM, SMEM, pl.BlockSpec((None, rows, columns), lambda i: (visit, 0, 0))],
            [
                pltpu.VMEM((slabs, rows + 2 * SUB, LANES), jnp.float32),
                pltpu.VMEM((NB, BR, BC), jnp.float32),
                pltpu.VMEM((devices, 2 * SUB, LANES), jnp.float32),
                pltpu.SMEM((devices * cap,), jnp.int32),
                pltpu.SMEM((devices,), jnp.int32),
                pltpu.SMEM((NB,), jnp.int32),
                pltpu.SemaphoreType.DMA((NB + 1,)),
            ],
            40 * pixels,
            4 * pixels * 3,
            grid=(1,),
            room=0 if visit == 0 else 16,
            out=VMEM if paired else pl.BlockSpec(memory_space=pltpu.HBM),
        )(own, targets, lanczos_shift, lanczos_frac, exposures)

    def exchanged(chunks):
        if len(chunks) == 1:
            return [lax.all_to_all(chunks[0], "ccd", split_axis=0, concat_axis=0, tiled=True)]
        moved = [chunks[0]]
        for k in range(1, devices):
            moved.append(
                lax.ppermute(chunks[k], "ccd", [(i, i ^ k) for i in range(devices)])
            )
        return moved

    template_chunks = warped(0, False)
    science_chunks = warped(1, paired)
    template_in = exchanged(template_chunks)
    science_in = exchanged(science_chunks)

    block_ids = jnp.arange(NB)
    earlier = block_ids[None, :] < block_ids[:, None]
    same = targets[:, :, None] == targets[:, None, :]
    order = jnp.sum(same & earlier[None], axis=2)
    in_place = order[:, None, :] == jnp.arange(cap)[None, :, None]

    def slots_at(patch):
        arrives = (targets == patch)[:, None, :] & in_place
        slots = jnp.sum(jnp.where(arrives, margin_slot[:, None, :], 0), axis=2)
        return jnp.where(jnp.any(arrives, axis=2), slots, NB).astype(jnp.int32)

    table = slots_at(owner).reshape(-1)
    wanted = jnp.arange(REACH * slabs)[:, None, None, None]
    row_of = jnp.arange(SUB // REACH * REACH).reshape(1, 1, SUB // REACH, REACH) % REACH
    spare = ((0, 0), (0, SUB // REACH - cap))

    def edge_rows(patch, first_slot):
        slots = jnp.pad(slots_at(patch), spare, constant_values=NB)
        slots = slots[None, :, :, None]
        hit = (slots - first_slot == wanted % slabs) & (row_of == wanted // slabs)
        return hit.astype(jnp.float32).reshape(REACH * slabs, devices * SUB)

    edges = jnp.stack([edge_rows(owner - 1, NB - slabs), edge_rows(owner + 1, 0)])

    sums = pltpu.VMEM((NB + 1, BR, BC), jnp.float32)
    size = NB
    count, coef = gram_table()
    at_ends = jnp.stack([owner == 0, owner == devices - 1]).astype(jnp.int32)
    shifts, gram = call(
        functools.partial(template_kernel, devices, cap, False),
        [f32(KSIDE, slabs, rows + 2 * SUB, LANES), f32(size, LANES)],
        [SMEM, SMEM, SMEM] + [VMEM] * (2 + len(template_in)),
        [
            sums,
            pltpu.VMEM((len(LAGS) - KSIDE, slabs, rows + 2 * SUB, LANES), jnp.float32),
            pltpu.VMEM((count, SUB, LANES), jnp.float32),
            pltpu.VMEM((count, SUB, LANES), jnp.float32),
        ],
        pixels * 2 * len(PRODUCTS),
        pixels * 8,
    )(own, table, at_ends, edges, jnp.asarray(coef), *template_in)

    first = devices - LATE if paired else len(science_in)
    science, sums = call(
        functools.partial(science_kernel, devices, cap, paired),
        [f32(NB + 1, BR, BC), f32(size, SUB, LANES)],
        [SMEM, SMEM, VMEM] + [VMEM] * first,
        [],
        pixels * 2 * KB,
        pixels * 16,
    )(own, table, shifts, *science_in[:first])
    if paired:
        science, fit = call(
            functools.partial(late_kernel, first, cap),
            [f32(NB + 1, BR, BC), f32(devices, SUB, LANES)],
            [SMEM, SMEM] + [VMEM] * (4 + LATE),
            [pltpu.VMEM((size, SUB, LANES), jnp.float32)],
            pixels * KB // 2,
            pixels * 8,
        )(own, table, shifts, gram, science, sums, *science_in[first:])
    else:
        fit = call(fit_kernel, f32(devices, SUB, LANES), [VMEM] * 2, [], 10**5, 10**5)(gram, sums)
    fit = lax.all_to_all(fit, "ccd", split_axis=0, concat_axis=0, tiled=True)

    return call(
        difference_kernel,
        f32(rows, columns),
        [VMEM] * 3,
        [pltpu.VMEM((rows, columns), jnp.float32), pltpu.SemaphoreType.DMA((rows // BR,))],
        pixels * 2 * KB,
        pixels * 12,
        out=pl.BlockSpec(memory_space=pltpu.HBM),
    )(fit, shifts, science)


def solution(mesh):
    placed = (
        P(None, ("field", "ccd"), None),
        P(None, ("field", "ccd"), None),
        P(None, ("field", "ccd"), None),
        P("field", None, None),
        P("field", None),
    )
    return jax.shard_map(
        body, mesh=mesh, in_specs=placed, out_specs=P(("field", "ccd"), None), check_vma=False
    )
```

```python
import functools

import jax
import jax.numpy as jnp
import numpy as np
from jax import lax
from jax.experimental import pallas as pl
from jax.experimental.pallas import tpu as pltpu
from jax.sharding import PartitionSpec as P


BR = 32
BC = 128
KSIDE = 5
KB = 25
NB = 32
REACH = KSIDE // 2
SUB = 8
LANES = 128
TAP_LOW, TAP_HIGH = -4, 5
TAPS = tuple(range(TAP_LOW, TAP_HIGH + 1))
LAGS = tuple(range(-(KSIDE - 1), KSIDE))
PRODUCTS = tuple(
    (down, lag) for down in range(KSIDE) for lag in (range(KSIDE) if down == 0 else LAGS)
)
EDGE_ROWS = ((0, (0, 1)), (1, (0,)), (-2, (0, 1)), (-1, (0,)))
EDGES = tuple(
    (row, down, lag) for row, downs in EDGE_ROWS for down, lag in PRODUCTS if down in downs
)
MAX_PERMUTES = 32
UNROLL = 4
STEP = 4
GROUP = 13
LATE = 2
RHS_LANE = KB


HIGHEST = lax.Precision.HIGHEST
SMEM = pl.BlockSpec(memory_space=pltpu.SMEM)
VMEM = pl.BlockSpec(memory_space=pltpu.VMEM)


def mm(a, b, contract=((1,), (0,))):
    return lax.dot_general(
        a, b, (contract, ((), ())), precision=HIGHEST, preferred_element_type=jnp.float32
    )


def call(kernel, out_shape, in_specs, scratch, flops, moved, grid=(), room=16, out=VMEM):
    many = isinstance(out_shape, (list, tuple))
    return pl.pallas_call(
        kernel,
        out_shape=out_shape,
        grid=grid,
        in_specs=in_specs,
        out_specs=[out] * len(out_shape) if many else out,
        scratch_shapes=scratch,
        cost_estimate=pl.CostEstimate(flops=flops, bytes_accessed=moved, transcendentals=0),
        compiler_params=pltpu.CompilerParams(vmem_limit_bytes=room << 20 if room else None),
    )


def f32(*shape):
    return jax.ShapeDtypeStruct(shape, jnp.float32)


def lane_ids():
    return lax.broadcasted_iota(jnp.int32, (SUB, LANES), 1)


def shifted(parts, by, lane):
    if by == 0:
        return list(parts)
    turned = [pltpu.roll(part, by % LANES, 1) for part in parts]
    zero = jnp.zeros_like(parts[0])
    out = []
    for j in range(len(parts)):
        beside = j - 1 if by > 0 else j + 1
        other = turned[beside] if 0 <= beside < len(parts) else zero
        keep = lane >= by if by > 0 else lane < LANES + by
        out.append(jnp.where(keep, turned[j], other))
    return out


def sinc(t):
    scaled = jnp.float32(np.pi) * t
    safe = jnp.where(t == 0.0, jnp.float32(1.0), scaled)
    return jnp.where(t == 0.0, jnp.float32(1.0), jnp.sin(safe) / safe)


def tap_weights(shift, frac, lane):
    t = (lane + TAP_LOW).astype(jnp.float32) - shift.astype(jnp.float32) - frac
    w = jnp.where(jnp.abs(t) < 3.0, sinc(t) * sinc(t / 3.0), 0.0)
    return [jnp.broadcast_to(w[:, k : k + 1], (SUB, LANES)) for k in range(len(TAPS))]


def warp_kernel(
    visit, devices, cap, paired, own_ref, tgt_ref, shift_ref, frac_ref, x_ref, *refs
):
    outs, (mid, blocks, edges, inv, cnt, where, sems) = refs[:-7], refs[-7:]
    rows, columns = x_ref.shape
    slabs, tiles = columns // LANES, rows // SUB
    own = own_ref[0]
    lane = lane_ids()

    for e in range(devices * cap):
        inv[e] = 0
    for p in range(devices):
        cnt[p] = 0

    def book(b):
        p = tgt_ref[own, b]
        c = cnt[p]
        cnt[p] = c + 1
        k = jnp.bitwise_xor(p, own) if paired else p
        at = k * cap + jnp.minimum(c, cap - 1)
        inv[at] = b
        where[b] = at

    col_w = tap_weights(shift_ref[visit, 0, 1], frac_ref[visit, 0, 1], lane)
    row_w = tap_weights(shift_ref[visit, 0, 0], frac_ref[visit, 0, 0], lane)
    for j in range(slabs):
        mid[j, 0:SUB, :] = jnp.zeros((SUB, LANES), jnp.float32)
        mid[j, SUB + rows :, :] = jnp.zeros((SUB, LANES), jnp.float32)

    def column_pass(t):
        for b in range(NB // tiles):
            book(t * (NB // tiles) + b)
        at = pl.multiple_of(t * SUB, SUB)
        parts = [x_ref[pl.ds(at, SUB), j * LANES : (j + 1) * LANES] for j in range(slabs)]
        zero = jnp.zeros((SUB, LANES), jnp.float32)
        ahead = [shifted([zero] + parts, -b, lane) for b in range(STEP)]
        total = [zero] * slabs
        for a in sorted({d // STEP for d in TAPS}):
            group = [zero] * (slabs + 1)
            for n, d in enumerate(TAPS):
                if d // STEP == a:
                    group = [g + col_w[n] * m for g, m in zip(group, ahead[d - STEP * a])]
            moved = shifted(group, -STEP * a, lane)[1:]
            total = [x + m for x, m in zip(total, moved)]
        for j in range(slabs):
            mid[j, pl.ds(at + SUB, SUB), :] = total[j]

    @pl.loop(0, rows // BR)
    def _(band):
        for t in range(BR // SUB):
            column_pass(band * (BR // SUB) + t)

    def send(b):
        p, r = lax.div(where[b], cap), lax.rem(where[b], cap)
        to = outs[0].at[p, pl.ds(pl.multiple_of(r * BR, BR), BR), :]
        return pltpu.make_async_copy(blocks.at[b], to, sems.at[b])

    @pl.loop(0, slabs)
    def _(j):
        for t in range(tiles):
            first = SUB + t * SUB
            total = jnp.zeros((SUB, LANES), jnp.float32)
            for n, d in enumerate(TAPS):
                total = total + row_w[n] * mid[j, first + d : first + d + SUB, :]
            inner = (t * SUB) % BR
            blocks[(t * SUB) // BR * slabs + j, inner : inner + SUB, :] = total
        if not paired:
            for band in range(rows // BR):
                send(band * slabs + j).start()

    if paired:
        for k in range(devices):
            for r in range(cap):
                outs[k][r * BR : (r + 1) * BR, :] = blocks[inv[k * cap + r]]
        return

    @pl.loop(0, devices, unroll=UNROLL)
    def _(p):
        before, after = jnp.maximum(p - 1, 0), jnp.minimum(p + 1, devices - 1)
        edges[p] = jnp.zeros((2 * SUB, LANES), jnp.float32)
        for r in range(cap):
            at = REACH * r
            edges[p, at : at + REACH, :] = blocks[inv[before * cap + r], BR - REACH : BR, :]
            at = SUB + REACH * r
            edges[p, at : at + REACH, :] = blocks[inv[after * cap + r], 0:REACH, :]

    last = pltpu.make_async_copy(edges, outs[0].at[:, cap * BR :, :], sems.at[NB])
    last.start()
    last.wait()

    @pl.loop(0, NB)
    def _(b):
        send(b).wait()


def sum_blocks(devices, cap, partners, own, table_ref, ins, acc):
    acc[...] = jnp.zeros_like(acc)

    def add(chunk, c):
        for r in range(cap):
            slot = table_ref[c * cap + r]
            acc[slot] = acc[slot] + chunk[r * BR : (r + 1) * BR, :]

    if partners:
        for k, chunk in zip(partners, ins):
            add(chunk, jnp.bitwise_xor(own, k))
    else:

        @pl.loop(0, devices)
        def _(c):
            add(ins[0].at[c], c)


def template_kernel(
    devices, cap, own_ref, table_ref, ends_ref, edges_ref, coef_ref, *refs
):
    ins, (cols_ref, gram_ref, acc, far, gen, spec) = refs[:-6], refs[-6:]
    slabs, rows = cols_ref.shape[1], cols_ref.shape[2] - 2 * SUB
    ext_ref = cols_ref.at[REACH]

    def lagged(lag):
        if abs(lag) <= REACH:
            return cols_ref.at[REACH - lag]
        return far.at[lag + KSIDE - 1 if lag < 0 else lag + KSIDE - 1 - KSIDE]

    tiles = rows // SUB
    lane = lane_ids()
    sub = lax.broadcasted_iota(jnp.int32, (SUB, LANES), 0)
    sum_blocks(devices, cap, (), own_ref[0], table_ref, ins, acc)

    for end in range(2):
        at = cap * BR + end * SUB
        strip = ins[0][:, at : at + SUB, :].reshape(devices * SUB, LANES)
        edge = mm(edges_ref[end], strip)
        first = SUB - REACH if end == 0 else SUB + rows
        for j in range(slabs):
            whole = 0 if end == 0 else SUB + rows
            ext_ref[j, whole : whole + SUB, :] = jnp.zeros((SUB, LANES), jnp.float32)
            for i in range(REACH):
                ext_ref[j, first + i : first + i + 1, :] = edge[i * slabs + j : i * slabs + j + 1]

    def lag_tile(parts, at):
        for lag in LAGS:
            for j, moved in enumerate(shifted(parts, lag, lane)):
                lagged(lag)[j, at, :] = moved

    for at in (slice(0, SUB), slice(SUB + rows, 2 * SUB + rows)):
        lag_tile([ext_ref[j, at, :] for j in range(slabs)], at)
    for band in range(rows // BR):

        @pl.loop(0, BR // SUB, unroll=UNROLL)
        def _(t):
            at = pl.ds(pl.multiple_of(t * SUB, SUB), SUB)
            to = pl.ds(pl.multiple_of(SUB + band * BR + t * SUB, SUB), SUB)
            parts = [acc[band * slabs + j, at, :] for j in range(slabs)]
            lag_tile(parts, to)

    gen[...] = jnp.zeros_like(gen)
    spec[...] = jnp.zeros_like(spec)

    @pl.loop(0, slabs)
    def _(j):
        def first(t, down, lag):
            base = SUB + t * SUB - down // 2
            return lagged(lag)[j, base : base + SUB, :]

        def second(t, down):
            base = SUB + t * SUB + down
            return ext_ref[j, base : base + SUB, :]

        sums = [None] * len(PRODUCTS)
        for t in range(tiles):
            moved = [second(t, down - down // 2) for down in range(KSIDE)]
            for n, (down, lag) in enumerate(PRODUCTS):
                term = first(t, down, lag) * moved[down]
                sums[n] = term if sums[n] is None else sums[n] + term
        edge = ((j == 0) & (lane < REACH)) | ((j == slabs - 1) & (lane >= LANES - REACH))
        for n in range(len(PRODUCTS)):
            gen[n] = gen[n] + jnp.where(edge, 0.0, sums[n])
            spec[n] = spec[n] + jnp.where(edge, sums[n], 0.0)
        for m, (row, down, lag) in enumerate(EDGES):
            n = len(PRODUCTS) + m
            t = 0 if row >= 0 else tiles - 1
            here = (sub == row % SUB) & (ends_ref[0 if row >= 0 else 1] > 0)
            term = first(t, 0, lag) * second(t, down)
            term = jnp.where(here, term, 0.0)
            gen[n] = gen[n] + jnp.where(edge, 0.0, term)
            spec[n] = spec[n] + jnp.where(edge, term, 0.0)

    src = lax.broadcasted_iota(jnp.int32, (LANES, LANES), 0)
    q2 = lax.rem(lax.broadcasted_iota(jnp.int32, (LANES, LANES), 1), KSIDE)
    late = (src >= REACH) & (q2 - REACH >= src - (LANES - 1))
    inside = jnp.where(((src < REACH) & (q2 - REACH <= src)) | late, 1.0, 0.0)
    data = mm(jnp.sum(gen[...], axis=1), jnp.ones((LANES, LANES), jnp.float32))
    data = data + mm(jnp.sum(spec[...], axis=1), inside)
    gram_ref[...] = jnp.zeros_like(gram_ref)
    for i in range(KB):
        gram_ref[i : i + 1, :] = jnp.sum(coef_ref[i] * data, axis=0, keepdims=True)
    total = gram_ref[...]
    size = total.shape[0]
    below = jnp.zeros((LANES - size, LANES), jnp.float32)
    flipped = jnp.transpose(jnp.concatenate([total, below], axis=0))[:size]
    row = lax.broadcasted_iota(jnp.int32, (size, LANES), 0)
    column = lax.broadcasted_iota(jnp.int32, (size, LANES), 1)
    gram_ref[...] = total + jnp.where(row == column, 0.0, flipped)


def joined_fit(gram, sums):
    rhs = jnp.sum(jnp.sum(sums, axis=1), axis=1, keepdims=True)
    size = gram.shape[0]
    column = lax.broadcasted_iota(jnp.int32, (size, LANES), 1)
    joined = jnp.where(column == RHS_LANE, rhs, gram)
    packed = joined[0:SUB]
    for a in range(1, size // SUB):
        packed = packed + pltpu.roll(joined[a * SUB : (a + 1) * SUB], a * size, 1)
    return packed


def science_kernel(devices, cap, partners, own_ref, table_ref, cols_ref, *refs):
    ins, (out, sums_ref) = refs[:-2], refs[-2:]
    slabs, rows = cols_ref.shape[1], cols_ref.shape[2] - 2 * SUB
    sum_blocks(devices, cap, partners, own_ref[0], table_ref, ins, out)
    sums_ref[...] = jnp.zeros_like(sums_ref)

    @pl.loop(0, slabs)
    def _(j):
        sums = [None] * KB
        for t in range(rows // SUB):
            base = SUB + t * SUB - REACH
            inner = (t * SUB) % BR
            target = out[(t * SUB) // BR * slabs + j, inner : inner + SUB, :]
            for r in range(KSIDE):
                for q in range(KSIDE):
                    i = r * KSIDE + q
                    term = cols_ref[q, j, base + r : base + r + SUB, :] * target
                    sums[i] = term if sums[i] is None else sums[i] + term
        for i in range(KB):
            sums_ref[i] = sums_ref[i] + sums[i]


def late_kernel(
    partners, cap, own_ref, table_ref, cols_ref, gram_ref, early_ref, sums_ref, *refs
):
    ins, (out, fit_ref, all_sums) = refs[:-3], refs[-3:]
    slabs = cols_ref.shape[1]
    out[...] = early_ref[...]
    sums = [sums_ref[i] for i in range(KB)]
    for k, chunk in zip(partners, ins):
        for r in range(cap):
            slot = table_ref[jnp.bitwise_xor(own_ref[0], k) * cap + r]
            out[slot] = out[slot] + chunk[r * BR : (r + 1) * BR, :]
            share = (slot < NB).astype(jnp.float32)
            inside = jnp.minimum(slot, NB - 1)
            j, band = lax.rem(inside, slabs), lax.div(inside, slabs)
            for t in range(BR // SUB):
                at = r * BR + t * SUB
                target = chunk[at : at + SUB, :] * share
                base = band * BR + SUB + t * SUB - REACH
                for i in range(KB):
                    part = cols_ref[i % KSIDE, j, pl.ds(base + i // KSIDE, SUB), :]
                    sums[i] = sums[i] + part * target
    all_sums[...] = jnp.zeros_like(all_sums)
    for i in range(KB):
        all_sums[i] = sums[i]
    packed = joined_fit(gram_ref[...], all_sums[...])
    for k in range(fit_ref.shape[0]):
        fit_ref[k] = packed


def fit_kernel(gram_ref, sums_ref, fit_ref):
    packed = joined_fit(gram_ref[...], sums_ref[...])
    for k in range(fit_ref.shape[0]):
        fit_ref[k] = packed


def solved(packed, size):
    parts = [packed] + [
        pltpu.roll(packed, LANES - a * size, 1) for a in range(1, size // SUB)
    ]
    work = jnp.concatenate(parts, axis=0)
    row = lax.broadcasted_iota(jnp.int32, (size, LANES), 0)
    lane = lax.broadcasted_iota(jnp.int32, (size, LANES), 1)
    diagonal = (row == lane) & (row < KB)
    trace = jnp.sum(jnp.where(diagonal, work, 0.0), axis=(0, 1), keepdims=True)
    ridge = 0.001 * trace / KB + 1.0
    work = jnp.where(lane < size, jnp.where(diagonal, work + ridge, work), 0.0)
    for base in range(0, KB, GROUP):
        group = [
            jnp.broadcast_to(work[:, i : i + 1], (size, LANES))
            for i in range(base, min(base + GROUP, KB))
        ]
        for k, column in enumerate(group):
            i = base + k
            inverse = 1.0 / column[i : i + 1]

            def eliminated(values):
                pivot = values[i : i + 1] * inverse
                return jnp.where(row == i, pivot, values - column * pivot)

            group[k + 1 :] = [eliminated(c) for c in group[k + 1 :]]
            work = eliminated(work)
    return work[:, RHS_LANE : RHS_LANE + 1]


def difference_kernel(fit_ref, cols_ref, sci_ref, out_ref, whole, sems):
    slabs, rows = cols_ref.shape[1], cols_ref.shape[2] - 2 * SUB
    shared = fit_ref[0]
    for k in range(1, fit_ref.shape[0]):
        shared = shared + fit_ref[k]
    kernel = solved(shared, NB)
    taps = [jnp.broadcast_to(kernel[i : i + 1, :], (SUB, LANES)) for i in range(KB)]

    def store(band):
        at = pl.ds(pl.multiple_of(band * BR, BR), BR)
        return pltpu.make_async_copy(whole.at[at, :], out_ref.at[at, :], sems.at[band])

    @pl.loop(0, rows // BR)
    def _(band):
        for j in range(slabs):
            for t in range(BR // SUB):
                total = None
                for r in range(KSIDE):
                    for q in range(KSIDE):
                        at = pl.ds(band * BR + SUB + t * SUB + r - REACH, SUB)
                        term = taps[r * KSIDE + q] * cols_ref[q, j, at, :]
                        total = term if total is None else total + term
                science = sci_ref[band * slabs + j, t * SUB : (t + 1) * SUB, :]
                at = pl.ds(pl.multiple_of(band * BR + t * SUB, SUB), SUB)
                whole[at, j * LANES : (j + 1) * LANES] = science - total
        store(band).start()

    for band in range(rows // BR):
        store(band).wait()


def by_permutes(devices):
    return devices <= MAX_PERMUTES and devices & (devices - 1) == 0


def exchange_order(devices):
    return tuple(range(1, devices))


def gram_table():
    count = -(-(len(PRODUCTS) + len(EDGES)) // SUB) * SUB
    coef = np.zeros((KB, count, LANES), np.float32)
    left_out = {0: (-2, -1), 1: (-1,), 2: (), 3: (0,), 4: (0, 1)}
    for r in range(KSIDE):
        for q in range(KSIDE):
            for n, (row, down, lag) in enumerate([(None, *p) for p in PRODUCTS] + list(EDGES)):
                if r + down < KSIDE and 0 <= q + lag < KSIDE:
                    column = (r + down) * KSIDE + q + lag
                    if row is None:
                        coef[r * KSIDE + q, n, column] = 1.0
                    elif row in left_out[r]:
                        coef[r * KSIDE + q, n, column] = -1.0
    return count, coef


def body(exposures, lanczos_shift, lanczos_frac, margin_patch, margin_slot):
    rows, columns = exposures.shape[1], exposures.shape[2]
    slabs = columns // LANES
    devices = lax.axis_size("ccd")
    owner = lax.axis_index("ccd")
    cap = max(2, 2 * NB // devices)
    paired = by_permutes(devices)
    own = owner.astype(jnp.int32).reshape(1)
    targets = margin_patch[:, :, 0]

    pixels = rows * columns

    def warped(visit, paired):
        packed = [f32(cap * BR, BC)] * devices if paired else [f32(devices, cap * BR + 2 * SUB, BC)]
        return call(
            functools.partial(warp_kernel, visit, devices, cap, paired),
            packed,
            [SMEM, SMEM, SMEM, SMEM, pl.BlockSpec((None, rows, columns), lambda i: (visit, 0, 0))],
            [
                pltpu.VMEM((slabs, rows + 2 * SUB, LANES), jnp.float32),
                pltpu.VMEM((NB, BR, BC), jnp.float32),
                pltpu.VMEM((devices, 2 * SUB, LANES), jnp.float32),
                pltpu.SMEM((devices * cap,), jnp.int32),
                pltpu.SMEM((devices,), jnp.int32),
                pltpu.SMEM((NB,), jnp.int32),
                pltpu.SemaphoreType.DMA((NB + 1,)),
            ],
            40 * pixels,
            4 * pixels * 3,
            grid=(1,),
            room=0 if visit == 0 else 16,
            out=VMEM if paired else pl.BlockSpec(memory_space=pltpu.HBM),
        )(own, targets, lanczos_shift, lanczos_frac, exposures)

    def exchanged(chunks):
        if len(chunks) == 1:
            return [lax.all_to_all(chunks[0], "ccd", split_axis=0, concat_axis=0, tiled=True)]
        moved = [chunks[0]]
        for k in range(1, devices):
            moved.append(
                lax.ppermute(chunks[k], "ccd", [(i, i ^ k) for i in range(devices)])
            )
        return moved

    template_chunks = warped(0, False)
    science_chunks = warped(1, paired)
    template_in = exchanged(template_chunks)
    science_in = exchanged(science_chunks)

    block_ids = jnp.arange(NB)
    earlier = block_ids[None, :] < block_ids[:, None]
    same = targets[:, :, None] == targets[:, None, :]
    order = jnp.sum(same & earlier[None], axis=2)
    in_place = order[:, None, :] == jnp.arange(cap)[None, :, None]

    def slots_at(patch):
        arrives = (targets == patch)[:, None, :] & in_place
        slots = jnp.sum(jnp.where(arrives, margin_slot[:, None, :], 0), axis=2)
        return jnp.where(jnp.any(arrives, axis=2), slots, NB).astype(jnp.int32)

    table = slots_at(owner).reshape(-1)
    wanted = jnp.arange(REACH * slabs)[:, None, None, None]
    row_of = jnp.arange(SUB // REACH * REACH).reshape(1, 1, SUB // REACH, REACH) % REACH
    spare = ((0, 0), (0, SUB // REACH - cap))

    def edge_rows(patch, first_slot):
        slots = jnp.pad(slots_at(patch), spare, constant_values=NB)
        slots = slots[None, :, :, None]
        hit = (slots - first_slot == wanted % slabs) & (row_of == wanted // slabs)
        return hit.astype(jnp.float32).reshape(REACH * slabs, devices * SUB)

    edges = jnp.stack([edge_rows(owner - 1, NB - slabs), edge_rows(owner + 1, 0)])

    sums = pltpu.VMEM((NB + 1, BR, BC), jnp.float32)
    size = NB
    count, coef = gram_table()
    at_ends = jnp.stack([owner == 0, owner == devices - 1]).astype(jnp.int32)
    shifts, gram = call(
        functools.partial(template_kernel, devices, cap),
        [f32(KSIDE, slabs, rows + 2 * SUB, LANES), f32(size, LANES)],
        [SMEM, SMEM, SMEM] + [VMEM] * (2 + len(template_in)),
        [
            sums,
            pltpu.VMEM((len(LAGS) - KSIDE, slabs, rows + 2 * SUB, LANES), jnp.float32),
            pltpu.VMEM((count, SUB, LANES), jnp.float32),
            pltpu.VMEM((count, SUB, LANES), jnp.float32),
        ],
        pixels * 2 * len(PRODUCTS),
        pixels * 8,
    )(own, table, at_ends, edges, jnp.asarray(coef), *template_in)

    order = (0, *exchange_order(devices)) if paired else ()
    early, late = (order[:-LATE], order[-LATE:]) if paired else ((), ())
    early_in = [science_in[k] for k in early] if paired else science_in
    science, sums = call(
        functools.partial(science_kernel, devices, cap, early),
        [f32(NB + 1, BR, BC), f32(size, SUB, LANES)],
        [SMEM, SMEM, VMEM] + [VMEM] * len(early_in),
        [],
        pixels * 2 * KB,
        pixels * 16,
    )(own, table, shifts, *early_in)
    if paired:
        science, fit = call(
            functools.partial(late_kernel, late, cap),
            [f32(NB + 1, BR, BC), f32(devices, SUB, LANES)],
            [SMEM, SMEM] + [VMEM] * (4 + LATE),
            [pltpu.VMEM((size, SUB, LANES), jnp.float32)],
            pixels * KB // 2,
            pixels * 8,
        )(own, table, shifts, gram, science, sums, *[science_in[k] for k in late])
    else:
        fit = call(fit_kernel, f32(devices, SUB, LANES), [VMEM] * 2, [], 10**5, 10**5)(gram, sums)
    fit = lax.all_to_all(fit, "ccd", split_axis=0, concat_axis=0, tiled=True)

    return call(
        difference_kernel,
        f32(rows, columns),
        [VMEM] * 3,
        [pltpu.VMEM((rows, columns), jnp.float32), pltpu.SemaphoreType.DMA((rows // BR,))],
        pixels * 2 * KB,
        pixels * 12,
        out=pl.BlockSpec(memory_space=pltpu.HBM),
    )(fit, shifts, science)


def solution(mesh):
    placed = (
        P(None, ("field", "ccd"), None),
        P(None, ("field", "ccd"), None),
        P(None, ("field", "ccd"), None),
        P("field", None, None),
        P("field", None),
    )
    return jax.shard_map(
        body, mesh=mesh, in_specs=placed, out_specs=P(("field", "ccd"), None), check_vma=False
    )
```
